128 devices in a mesh: cuts: 4 (over z), tile: 32 (over x, y, core).
Axes of the slice: x: 4, y: 4, z: 4, core: 2. Of those that a mesh axis runs over, the one named last changes fastest.
Arguments:
- probe_wave: float32 [2, 256, 256], replicated, may hold values from -6 to 6
- transmission: float32 [4, 2, 4096, 8192], P('cuts', None, None, 'tile'), may hold values from -1 to 1, as said below
- kernel_phase: float32 [256, 256], replicated, may hold values from -3.140625 to 3.140625
- measured: bfloat16 [32, 6, 256, 256], P('tile'), may hold values from 0 to 4
- counts: int32 [32], P('tile'), may hold values from 1 to 6, as said below
- positions: int32 [32, 6, 2], P('tile'), may hold values from 0 to 3840, as said below
- widths: int32 [32, 2], P('tile'), may hold values from 32 to 128
Outputs:
- adjoint_wave: float32 [4, 32, 6, 2, 256, 256], P('cuts', 'tile')
- object_grad: float32 [4, 2, 4096, 8192], P('cuts', None, None, 'tile')
The draws below stay inside these ranges and needn't reach their ends.
Inputs may be any that keep to these rules, and one draw needn't show every extreme that they name: Every entry has magnitude at most 1; each pair is a complex transmission. Tile t uses its first counts[t] slots; some tile uses all 6 slots. `positions`: rows lie in 0 to 3840 and columns in 0 to 256; column 0 of a tile's extended patch is 128 columns left of its first own column.
All inputs are finite; a program needn't handle non-finite values.
Results may differ from the reference program's by a relative error of at most 0.0003.
Values sent between devices are 32-bit elements; how exact they have to be, the bound alone decides.
No kernel may reach another device: no remote copies, remote signals or barrier semaphores. Data moves between devices by JAX's collectives and lax.ppermute only.
A program may use at most 256 MiB of HBM per device.

```python
import math
import jax
import jax.numpy as jnp
from jax import lax

W = 256
TH = 4096
TW = 256
RIM = 128
CAP = 6
SLICES = 1
GROUPS = 4
TILES = 32
NCOL = 8192
NSLICE = 4


def draw_transmission(key, part):
    key_amp, key_phase = jax.random.split(key, 2)
    shape_here = (NSLICE, TH, NCOL)
    amplitude = jax.random.uniform(key_amp, shape_here, jnp.float32, 0.85, 1.0)
    phases = jnp.clip(0.6 * jax.random.normal(key_phase, shape_here, jnp.float32), -1.5, 1.5)
    return jnp.stack([amplitude * jnp.cos(phases), amplitude * jnp.sin(phases)], axis=1)


def draw_counts(key, part):
    key_light = jax.random.fold_in(key, 11)
    key_heavy = jax.random.fold_in(key, 12)
    key_pick = jax.random.fold_in(key, 13)
    light_load = jax.random.randint(key_light, (TILES,), 1, 4)
    heavy_load = jax.random.randint(key_heavy, (TILES,), 0, 4) == 0
    chosen = jax.random.randint(key_pick, (), 0, TILES)
    filled = heavy_load | (jnp.arange(TILES, dtype=jnp.int32) == chosen)
    return jnp.where(filled, CAP, light_load).astype(jnp.int32)


def draw_positions(key, part):
    key_rows = jax.random.fold_in(key, 21)
    key_cols = jax.random.fold_in(key, 22)
    row_place = jax.random.randint(key_rows, (TILES, CAP), 0, TH - W + 1)
    col_place = jax.random.randint(key_cols, (TILES, CAP), 0, TW + 2 * RIM - W + 1)
    return jnp.stack([row_place, col_place], axis=-1).astype(jnp.int32)


def set_ends(values, stream_key, smallest, top_value):
    dims = values.shape
    place = [jax.random.randint(jax.random.fold_in(stream_key, axis), (), 0, dims[axis]) for axis in range(len(dims))]
    values = values.at[tuple(place)].set(smallest)
    longest = dims.index(max(dims))
    place[longest] = (place[longest] + 1) % dims[longest]
    return values.at[tuple(place)].set(top_value)


def shard_levels(stream_key, dims, cuts, smallest, high):
    def one(axis_at, blocks):
        steps = jax.random.uniform(jax.random.fold_in(jax.random.fold_in(stream_key, 6), axis_at), (blocks,), jnp.float32, smallest / len(cuts), high / len(cuts))
        return jnp.repeat(jnp.exp(steps), dims[axis_at] // blocks).reshape((-1,) + (1,) * (len(dims) - axis_at - 1))

    level = one(*cuts[0])
    for cut in cuts[1:]:
        level = level * one(*cut)
    return level


def normal_values(rng, dims, width, reach, kind=jnp.bfloat16):
    values = width * jax.random.normal(rng, dims, jnp.float32)
    return jnp.clip(values, min=-reach, max=reach).astype(kind)


def setup_inputs(seed: int = 0) -> dict:
    key_of = jax.random.split(jax.random.key(seed), 8)
    return {
        "probe_wave": normal_values(key_of[0], (2, W, W), 1.0, 6.0, jnp.float32),
        "transmission": draw_transmission(jax.random.fold_in(key_of[7], 71), 0),
        "kernel_phase": jnp.clip(jax.random.uniform(key_of[2], (W, W), jnp.float32, -3.140625, 3.140625), -3.140625, 3.140625),
        "measured": jnp.clip(4.0 * jax.random.uniform(key_of[3], (TILES, CAP, W, W), jnp.float32) ** shard_levels(key_of[3], (TILES, CAP, W, W), ((0, 32),), -0.2, 0.2), 0.0, 4.0).astype(jnp.bfloat16),
        "counts": draw_counts(jax.random.fold_in(key_of[7], 71), 0),
        "positions": draw_positions(jax.random.fold_in(key_of[7], 71), 0),
        "widths": set_ends(jax.random.randint(key_of[6], (TILES, 2), RIM // 4, RIM + 1), jax.random.fold_in(key_of[6], 1), RIM // 4, RIM).astype(jnp.int32),
    }


def make_tables():
    indices = jnp.arange(W, dtype=jnp.int32)
    product = indices[:, None] * indices[None, :] % W
    angles = product.astype(jnp.float32) * (2.0 * math.pi / W)
    cosine = jnp.cos(angles) / math.sqrt(W)
    sine_part = jnp.sin(angles) / math.sqrt(W)
    forward = jnp.concatenate([jnp.concatenate([cosine, sine_part], 1), jnp.concatenate([-sine_part, cosine], 1)], 0)
    inverse = jnp.concatenate([jnp.concatenate([cosine, -sine_part], 1), jnp.concatenate([sine_part, cosine], 1)], 0)
    return (forward, inverse)

def transform(fields, matrix):
    number = fields.shape[0]
    stacked = fields.reshape(number, 2 * W, W)
    halfway = jnp.einsum('ab,pbc->pac', matrix, stacked, precision=lax.Precision.HIGHEST)
    halfway = halfway.reshape(number, 2, W, W)
    quadrant = matrix.reshape(2, W, 2, W)
    return jnp.einsum('psik,rjsk->prij', halfway, quadrant, precision=lax.Precision.HIGHEST)

def complex_mul(first_op, second_op):
    first_re, first_im = (first_op[..., 0, :, :], first_op[..., 1, :, :])
    second_re, second_im = (second_op[..., 0, :, :], second_op[..., 1, :, :])
    return jnp.stack([first_re * second_re - first_im * second_im, first_re * second_im + first_im * second_re], axis=-3)

def conj_mul(first_op, second_op):
    first_re, first_im = (first_op[..., 0, :, :], first_op[..., 1, :, :])
    second_re, second_im = (second_op[..., 0, :, :], second_op[..., 1, :, :])
    return jnp.stack([first_re * second_re + first_im * second_im, first_re * second_im - first_im * second_re], axis=-3)

def propagate(fields, kernel, tables):
    spectrum = transform(fields, tables[0])
    return transform(complex_mul(kernel, spectrum), tables[1])

def keep_columns(tile_at, width_pair):
    columns = jnp.arange(TW + 2 * RIM, dtype=jnp.int32)
    globally = tile_at * TW - RIM + columns
    inside = (globally >= 0) & (globally < TILES * TW)
    middle = (columns >= RIM) & (columns < RIM + TW)
    left_ok = (columns < RIM) & (RIM - columns <= width_pair[0])
    right_ok = (columns >= RIM + TW) & (columns - RIM - TW + 1 <= width_pair[1])
    return inside & (middle | left_ok | right_ok)

def cut_windows(grad_plane, places):
    anchor = jnp.zeros((), jnp.int32)

    def single(corner):
        return lax.dynamic_slice(grad_plane, (anchor, corner[0], corner[1]), (2, W, W))
    return jax.vmap(single)(places)

def add_windows(grad_plane, places, contrib):
    anchor = jnp.zeros((), jnp.int32)
    for item_at in range(contrib.shape[0]):
        corner_at = (anchor, places[item_at, 0], places[item_at, 1])
        current = lax.dynamic_slice(grad_plane, corner_at, (2, W, W))
        grad_plane = lax.dynamic_update_slice(grad_plane, current + contrib[item_at], corner_at)
    return grad_plane

def reference(probe_wave, transmission, kernel_phase, measured, counts, positions, widths):
    tables = make_tables()
    kernel = jnp.stack([jnp.cos(kernel_phase), jnp.sin(kernel_phase)], 0)
    kernel_conj = jnp.stack([jnp.cos(kernel_phase), -jnp.sin(kernel_phase)], 0)
    padded = jnp.pad(transmission, ((0, 0), (0, 0), (0, 0), (RIM, RIM)))
    vacuum = jnp.array([1.0, 0.0], dtype=jnp.float32)[:, None, None]

    def one_tile(operands):
        tile_at, count_here, places, width_pair, observed = operands
        keep_mask = keep_columns(tile_at, width_pair)
        object_patch = lax.dynamic_slice_in_dim(padded, tile_at * TW, TW + 2 * RIM, 3)
        object_patch = jnp.where(keep_mask, object_patch, vacuum)
        live_slots = (jnp.arange(CAP, dtype=jnp.int32) < count_here).astype(jnp.float32)
        fields = probe_wave[None] * live_slots[:, None, None, None]
        saved_waves = []
        window_list = []
        for slice_at in range(NSLICE):
            windows = cut_windows(object_patch[slice_at], places)
            saved_waves.append(fields)
            window_list.append(windows)
            fields = propagate(complex_mul(windows, fields), kernel, tables)
        far_field = transform(fields, tables[0])
        intensity = far_field[:, 0] * far_field[:, 0] + far_field[:, 1] * far_field[:, 1]
        residual = intensity - observed.astype(jnp.float32)
        backward = transform(far_field * residual[:, None], tables[1])
        grad_list = []
        entry_list = [None] * GROUPS
        for slice_at in reversed(range(NSLICE)):
            turned = propagate(backward, kernel_conj, tables)
            contrib = conj_mul(saved_waves[slice_at], turned)
            grad_plane = add_windows(jnp.zeros_like(object_patch[slice_at]), places, contrib)
            grad_list.insert(0, jnp.where(keep_mask, grad_plane, 0.0))
            backward = conj_mul(window_list[slice_at], turned)
            if slice_at % SLICES == 0:
                entry_list[slice_at // SLICES] = backward
        grad_patch = jnp.stack(grad_list, 0)
        return (jnp.stack(entry_list, 0), grad_patch[..., :RIM], grad_patch[..., RIM:RIM + TW], grad_patch[..., RIM + TW:])
    tile_ids = jnp.arange(TILES, dtype=jnp.int32)
    entries, left_rims, center, right_rims = lax.map(one_tile, (tile_ids, counts, positions, widths, measured))
    from_left = jnp.concatenate([jnp.zeros_like(right_rims[:1]), right_rims[:-1]], 0)
    from_right = jnp.concatenate([left_rims[1:], jnp.zeros_like(left_rims[:1])], 0)
    center = center.at[..., :RIM].add(from_left)
    center = center.at[..., TW - RIM:].add(from_right)
    object_grad = jnp.moveaxis(center, 0, 3).reshape(NSLICE, 2, TH, NCOL)
    adjoint_wave = jnp.swapaxes(entries, 0, 1)
    return (adjoint_wave, object_grad)
```

```python
import math

import jax
import jax.numpy as jnp
import ml_dtypes
import numpy as np
from jax import lax
from jax.experimental import pallas as pl
from jax.experimental.pallas import tpu as pltpu
from jax.sharding import PartitionSpec as P

RIM = 128
HALF = 128
W = 256
F32 = jnp.float32
BF16 = jnp.bfloat16
VMEM_BYTES = 56 * 1024 * 1024

ANY_SPEC = pl.BlockSpec(memory_space=pl.ANY)
SMEM_SPEC = pl.BlockSpec(memory_space=pltpu.SMEM)
VMEM_SPEC = pl.BlockSpec(memory_space=pltpu.VMEM)


def split_table(table):
    high = table.astype(ml_dtypes.bfloat16)
    low = (table - high.astype(np.float64)).astype(ml_dtypes.bfloat16)
    return high, low


def make_tables():
    freq = np.arange(HALF)[:, None]
    place = np.arange(HALF)[None, :]
    out = []
    for odd in (0, 1):
        angle = 2.0 * math.pi * (((2 * freq + odd) * place) % W) / W
        re, im = np.cos(angle) / math.sqrt(W), -np.sin(angle) / math.sqrt(W)
        real = np.block([[re, -im], [im, re]])
        out += [*split_table(real), *split_table(real.T)]
    return np.stack(out)


def make_order():
    order = np.concatenate([np.arange(0, W, 2), np.arange(1, W, 2)])
    hot = np.zeros((W, W), np.float32)
    hot[np.arange(W), order] = 1.0
    return hot


TABLES = make_tables()
ORDER = make_order()


def dot(first, second):
    return jnp.dot(first, second, preferred_element_type=F32)


def split(value):
    high = value.astype(BF16)
    return high, (value - high.astype(F32)).astype(BF16)


def table_left(tab, at, value):
    high, low = split(value)
    return dot(tab[at], high) + dot(tab[at], low) + dot(tab[at + 1], high)


def table_right(value, tab, at):
    high, low = split(value)
    return dot(high, tab[at]) + dot(low, tab[at]) + dot(high, tab[at + 1])


def to_spectrum(re, im, tab):
    h = HALF
    total = jnp.concatenate([re[:h] + re[h:], im[:h] + im[h:]], 0)
    diff = jnp.concatenate([re[:h] - re[h:], im[:h] - im[h:]], 0)
    even = table_left(tab, 0, total)
    odd = table_left(tab, 4, diff)
    yr = jnp.concatenate([even[:h], odd[:h]], 0)
    yi = jnp.concatenate([even[h:], odd[h:]], 0)
    total = jnp.concatenate([yr[:, :h] + yr[:, h:], yi[:, :h] + yi[:, h:]], 1)
    diff = jnp.concatenate([yr[:, :h] - yr[:, h:], yi[:, :h] - yi[:, h:]], 1)
    return table_right(total, tab, 2), table_right(diff, tab, 6)


def from_spectrum(even, odd, tab):
    h = HALF
    a = table_right(even, tab, 0)
    b = table_right(odd, tab, 4)
    yr = jnp.concatenate([a[:, :h] + b[:, :h], a[:, :h] - b[:, :h]], 1)
    yi = jnp.concatenate([a[:, h:] + b[:, h:], a[:, h:] - b[:, h:]], 1)
    p = table_left(tab, 2, jnp.concatenate([yr[:h], yi[:h]], 0))
    q = table_left(tab, 6, jnp.concatenate([yr[h:], yi[h:]], 0))
    re = jnp.concatenate([p[:h] + q[:h], p[:h] - q[:h]], 0)
    im = jnp.concatenate([p[h:] + q[h:], p[h:] - q[h:]], 0)
    return re, im


def turn(spectrum, cosine, sine):
    h = HALF
    re, im = spectrum[:, :h], spectrum[:, h:]
    return jnp.concatenate([re * cosine - im * sine, re * sine + im * cosine], 1)


def propagate(re, im, kern, tab, sign):
    h = HALF
    even, odd = to_spectrum(re, im, tab)
    cosine, sine = kern[0], sign * kern[1]
    even = turn(even, cosine[:, :h], sine[:, :h])
    odd = turn(odd, cosine[:, h:], sine[:, h:])
    return from_spectrum(even, odd, tab)


def row_base(row):
    base = pl.multiple_of((row // 8) * 8, 8)
    extra = pl.multiple_of(jnp.minimum(base + W, 4096 - 8), 8)
    return base, extra, row - base


def rows_below(delta, shape):
    return lax.broadcasted_iota(jnp.int32, shape, len(shape) - 2) < delta


def cut_rims(cap):
    def kernel(pos_left, pos_right, image, to_left, to_right, extra, sems):
        copies = []
        for s in range(cap):
            for side, (pos, out, first) in enumerate(
                ((pos_left, to_left, 0), (pos_right, to_right, HALF))
            ):
                base, more, _ = row_base(pos[s, 0])
                cols = pl.ds(first, HALF)
                copies.append((
                    pltpu.make_async_copy(
                        image.at[:, pl.ds(base, W), cols], out.at[s], sems.at[2 * s + side, 0]
                    ),
                    pltpu.make_async_copy(
                        image.at[:, pl.ds(more, 8), cols],
                        extra.at[2 * s + side],
                        sems.at[2 * s + side, 1],
                    ),
                ))
        for pair in copies:
            for copy in pair:
                copy.start()
        for s in range(cap):
            for side, (pos, out) in enumerate(((pos_left, to_left), (pos_right, to_right))):
                for copy in copies[2 * s + side]:
                    copy.wait()
                delta = pos[s, 0] % 8
                mask = rows_below(delta, (2, 8, HALF))
                out[s, :, 0:8, :] = jnp.where(mask, extra[2 * s + side], out[s, :, 0:8, :])

    strips = jax.ShapeDtypeStruct((cap, 2, W, HALF), F32)
    return pl.pallas_call(
        kernel,
        out_shape=(strips, strips),
        in_specs=[SMEM_SPEC, SMEM_SPEC, ANY_SPEC],
        out_specs=(VMEM_SPEC, VMEM_SPEC),
        scratch_shapes=[
            pltpu.VMEM((2 * cap, 2, 8, HALF), F32),
            pltpu.SemaphoreType.DMA((2 * cap, 2)),
        ],
        compiler_params=pltpu.CompilerParams(vmem_limit_bytes=VMEM_BYTES),
        name="cut_rims",
    )


def slot_of(owner, second):
    return 4 + owner // 2 if second else owner


def make_windows():
    def kernel(meta, pos, image, from_left, from_right, *rest):
        outs, (extra, sems, rim_buf) = rest[:8], rest[8:]
        group, tile, parity = meta[0], meta[1], meta[2]
        wide_left, wide_right, tiles = meta[4], meta[5], meta[6]

        def job(at):
            second, k = divmod(at, 4)
            owner = (group + k) % 4
            valid = (owner % 2 == parity) if second else (owner >= 0)
            return slot_of(owner, second), valid

        def transfers(at, s):
            base, more, _ = row_base(pos[s, 0])
            return (
                pltpu.make_async_copy(image.at[:, pl.ds(base, W), :], outs[at], sems.at[at, 0]),
                pltpu.make_async_copy(
                    image.at[:, pl.ds(more, 8), :], extra.at[at], sems.at[at, 1]
                ),
                pltpu.make_async_copy(from_left.at[s], rim_buf.at[at, 0], sems.at[at, 2]),
                pltpu.make_async_copy(from_right.at[s], rim_buf.at[at, 1], sems.at[at, 3]),
            )

        for at in range(8):
            s, valid = job(at)

            @pl.when(valid)
            def _(at=at, s=s):
                for copy in transfers(at, s):
                    copy.start()

        for at in range(8):
            s, valid = job(at)

            @pl.when(valid)
            def _(at=at, s=s):
                for copy in transfers(at, s):
                    copy.wait()
                delta = pos[s, 0] % 8
                edge = pos[s, 1] - RIM
                out = outs[at]
                mask = rows_below(delta, (2, 8, W))
                out[:, 0:8, :] = jnp.where(mask, extra[at], out[:, 0:8, :])
                lane = lax.broadcasted_iota(jnp.int32, (W, HALF), 1)

                @pl.when(edge > 0)
                def _():
                    rim = lane < edge
                    kept = (lane < wide_right) & (tile < tiles - 1)
                    for part in range(2):
                        value = jnp.where(kept, rim_buf[at, 1, part], 1.0 - part)
                        out[part, :, :HALF] = jnp.where(rim, value, out[part, :, :HALF])

                @pl.when(edge < 0)
                def _():
                    rim = lane + HALF >= W + edge
                    kept = (lane + HALF >= W - wide_left) & (tile > 0)
                    for part in range(2):
                        value = jnp.where(kept, rim_buf[at, 0, part], 1.0 - part)
                        out[part, :, HALF:] = jnp.where(rim, value, out[part, :, HALF:])

    window = jax.ShapeDtypeStruct((2, W, W), F32)
    return pl.pallas_call(
        kernel,
        out_shape=(window,) * 8,
        in_specs=[SMEM_SPEC, SMEM_SPEC, ANY_SPEC, ANY_SPEC, ANY_SPEC],
        out_specs=(VMEM_SPEC,) * 8,
        scratch_shapes=[
            pltpu.VMEM((8, 2, 8, W), F32),
            pltpu.SemaphoreType.DMA((8, 4)),
            pltpu.VMEM((8, 2, 2, W, HALF), F32),
        ],
        compiler_params=pltpu.CompilerParams(vmem_limit_bytes=VMEM_BYTES),
        name="make_windows",
    )


def forward_slot(second):
    def kernel(meta, pos, probe, measured, kern, tab, order, order_t, *rest):
        wins, inputs, back = rest[:4], rest[4:8], rest[8]
        win_buf, in_buf, seen, sems = rest[9:]
        group, parity, live = meta[0], meta[2], meta[3]
        s = slot_of(group, second)
        valid = (group % 2 == parity) if second else (group >= 0)

        @pl.when(valid)
        def _():
            loads = []
            for k in range(4):
                n = (group - k) % 4
                loads.append(pltpu.make_async_copy(wins[k], win_buf.at[n], sems.at[k]))
            seeing = pltpu.make_async_copy(measured.at[s], seen, sems.at[4])
            for copy in loads:
                copy.start()
            seeing.start()
            down = pos[s, 0] % 8
            across = (pos[s, 1] - RIM) % W
            scale = jnp.where(s < live, 1.0, 0.0)
            for part in range(2):
                rolled = pltpu.roll(probe[part], across, 1)
                in_buf[0, part] = pltpu.roll(rolled, down, 0) * scale
            for copy in loads:
                copy.wait()

            def step(n, carry):
                re, im = in_buf[n, 0], in_buf[n, 1]
                wr, wi = win_buf[n, 0], win_buf[n, 1]
                re, im = wr * re - wi * im, wr * im + wi * re
                re, im = propagate(re, im, kern, tab, 1.0)
                in_buf[n + 1, 0] = re
                in_buf[n + 1, 1] = im
                return carry

            lax.fori_loop(0, 4, step, 0)
            stores = []
            for k in range(4):
                n = (group + k) % 4
                stores.append(pltpu.make_async_copy(in_buf.at[n], inputs[k], sems.at[5 + k]))
            for copy in stores:
                copy.start()
            seeing.wait()
            half_seen = dot(order[...], seen[...]).astype(BF16)
            target = dot(half_seen, order_t[...])
            spectra = to_spectrum(in_buf[4, 0], in_buf[4, 1], tab)
            chis = []
            for odd in range(2):
                re, im = spectra[odd][:, :HALF], spectra[odd][:, HALF:]
                rest_of = re * re + im * im - target[:, odd * HALF : (odd + 1) * HALF]
                chis.append(jnp.concatenate([re * rest_of, im * rest_of], 1))
            re, im = from_spectrum(chis[0], chis[1], tab)
            back[0] = re
            back[1] = im
            for copy in stores:
                copy.wait()

    field = jax.ShapeDtypeStruct((2, W, W), F32)
    return pl.pallas_call(
        kernel,
        out_shape=(field,) * 5,
        in_specs=[SMEM_SPEC, SMEM_SPEC, VMEM_SPEC, ANY_SPEC]
        + [VMEM_SPEC] * 4
        + [ANY_SPEC] * 4,
        out_specs=(ANY_SPEC,) * 4 + (VMEM_SPEC,),
        scratch_shapes=[
            pltpu.VMEM((4, 2, W, W), F32),
            pltpu.VMEM((5, 2, W, W), F32),
            pltpu.VMEM((W, W), BF16),
            pltpu.SemaphoreType.DMA((9,)),
        ],
        compiler_params=pltpu.CompilerParams(vmem_limit_bytes=VMEM_BYTES),
        name="forward_second" if second else "forward_first",
    )


def backward_slot(second):
    def kernel(meta, back, kern, tab, *rest):
        wins, turned = rest[:4], rest[4:8]
        win_buf, turned_buf, back_buf, sems = rest[8:]
        group, parity = meta[0], meta[2]
        valid = (group % 2 == parity) if second else (group >= 0)

        @pl.when(valid)
        def _():
            loads = []
            for k in range(4):
                n = (group - k) % 4
                loads.append(pltpu.make_async_copy(wins[k], win_buf.at[n], sems.at[k]))
            for copy in loads:
                copy.start()
            back_buf[...] = back[...]
            for copy in loads:
                copy.wait()

            def step(at, carry):
                n = 3 - at
                re, im = propagate(back_buf[0], back_buf[1], kern, tab, -1.0)
                turned_buf[n, 0] = re
                turned_buf[n, 1] = im
                wr, wi = win_buf[n, 0], win_buf[n, 1]
                back_buf[0] = wr * re + wi * im
                back_buf[1] = wr * im - wi * re
                return carry

            lax.fori_loop(0, 4, step, 0)
            stores = []
            for k in range(4):
                n = (group + k) % 4
                stores.append(pltpu.make_async_copy(turned_buf.at[n], turned[k], sems.at[4 + k]))
            for copy in stores:
                copy.start()
            for copy in stores:
                copy.wait()

    field = jax.ShapeDtypeStruct((2, W, W), F32)
    return pl.pallas_call(
        kernel,
        out_shape=(field,) * 4,
        in_specs=[SMEM_SPEC] + [VMEM_SPEC] * 3 + [ANY_SPEC] * 4,
        out_specs=(ANY_SPEC,) * 4,
        scratch_shapes=[
            pltpu.VMEM((4, 2, W, W), F32),
            pltpu.VMEM((4, 2, W, W), F32),
            pltpu.VMEM((2, W, W), F32),
            pltpu.SemaphoreType.DMA((8,)),
        ],
        compiler_params=pltpu.CompilerParams(vmem_limit_bytes=VMEM_BYTES),
        name="backward_second" if second else "backward_first",
    )


def slice_terms(second, cap):
    count = 2 if second else 4
    first = 4 if second else 0

    def kernel(meta, pos, probe, *rest):
        if second:
            rest = rest[1:]
        turned, inputs, wins = rest[:4], rest[4:8], rest[8:12]
        adjoint, own, to_left, to_right = rest[12:16]
        t_buf, i_buf, w_buf, a_buf, sems = rest[16:]
        group, tile, parity, live = meta[0], meta[1], meta[2], meta[3]
        wide_left, wide_right, tiles = meta[4], meta[5], meta[6]

        def job(j):
            owner = (group - j) % 4
            valid = (owner % 2 == parity) if second else (owner >= 0)
            return slot_of(owner, second), valid

        def loads(j):
            return (
                pltpu.make_async_copy(turned[j], t_buf.at[j], sems.at[j, 0]),
                pltpu.make_async_copy(inputs[j], i_buf.at[j], sems.at[j, 1]),
                pltpu.make_async_copy(wins[(4 - j) % 4], w_buf.at[j], sems.at[j, 2]),
            )

        def store(j, s):
            return pltpu.make_async_copy(a_buf.at[j], adjoint.at[s], sems.at[j, 3])

        for j in range(4):
            s, valid = job(j)

            @pl.when(valid)
            def _(j=j):
                for copy in loads(j):
                    copy.start()

        for j in range(4):
            s, valid = job(j)

            @pl.when(valid)
            def _(j=j, s=s):
                for copy in loads(j):
                    copy.wait()
                down = pos[s, 0] % 8
                edge = pos[s, 1] - RIM
                across = edge % W

                @pl.when(group == 0)
                def _():
                    scale = jnp.where(s < live, 1.0, 0.0)
                    for part in range(2):
                        rolled = pltpu.roll(probe[part], across, 1)
                        i_buf[j, part] = pltpu.roll(rolled, down, 0) * scale

                re, im = t_buf[j, 0], t_buf[j, 1]
                wr, wi = w_buf[j, 0], w_buf[j, 1]
                for part, value in enumerate((wr * re + wi * im, wr * im - wi * re)):
                    rolled = pltpu.roll(value, (W - across) % W, 1)
                    a_buf[j, part] = pltpu.roll(rolled, (W - down) % W, 0)
                store(j, s).start()
                lane = lax.broadcasted_iota(jnp.int32, (W, W), 1)
                rim_left = lane >= W + edge
                rim_right = lane < edge
                half = lax.broadcasted_iota(jnp.int32, (W, HALF), 1)
                sent_left = (half + HALF >= W + edge) & (half + HALF >= W - wide_left) & (tile > 0)
                sent_right = (half < edge) & (half < wide_right) & (tile < tiles - 1)
                ir, ii = i_buf[j, 0], i_buf[j, 1]
                at = s - first
                for part, value in enumerate((ir * re + ii * im, ir * im - ii * re)):
                    own[at, part] = jnp.where(rim_left | rim_right, 0.0, value)
                    to_left[at, part] = jnp.where(sent_left, value[:, HALF:], 0.0)
                    to_right[at, part] = jnp.where(sent_right, value[:, :HALF], 0.0)

        for j in range(4):
            s, valid = job(j)

            @pl.when(valid)
            def _(j=j, s=s):
                store(j, s).wait()

    waves = jax.ShapeDtypeStruct((cap, 2, W, W), F32)
    own = jax.ShapeDtypeStruct((count, 2, W, W), F32)
    strips = jax.ShapeDtypeStruct((count, 2, W, HALF), F32)
    extra = [ANY_SPEC] if second else []
    return pl.pallas_call(
        kernel,
        out_shape=(waves, own, strips, strips),
        in_specs=[SMEM_SPEC, SMEM_SPEC, VMEM_SPEC] + extra + [ANY_SPEC] * 12,
        out_specs=(ANY_SPEC, VMEM_SPEC, VMEM_SPEC, VMEM_SPEC),
        scratch_shapes=[pltpu.VMEM((4, 2, W, W), F32)] * 4 + [pltpu.SemaphoreType.DMA((4, 4))],
        input_output_aliases={3: 0} if second else {},
        compiler_params=pltpu.CompilerParams(vmem_limit_bytes=VMEM_BYTES),
        name="terms_second" if second else "terms_first",
    )


def add_terms(cap, rows):
    def kernel(pos, pos_left, pos_right, own1, own2, left1, left2, right1, right2, out):
        out[...] = jnp.zeros_like(out)

        def add(row, value, cols):
            base, more, delta = row_base(row)
            width = value.shape[-1]
            below = rows_below(delta, (W, width))
            few = rows_below(delta, (8, width))
            for part in range(2):
                out[part, pl.ds(base, W), cols] += jnp.where(below, 0.0, value[part])
                out[part, pl.ds(more, 8), cols] += jnp.where(few, value[part, :8], 0.0)

        for s in range(cap):
            pick = (lambda one, two: one[s] if s < 4 else two[s - 4])
            add(pos[s, 0], pick(own1, own2), slice(0, W))
            add(pos_left[s, 0], pick(left1, left2), slice(0, HALF))
            add(pos_right[s, 0], pick(right1, right2), slice(HALF, W))

    return pl.pallas_call(
        kernel,
        out_shape=jax.ShapeDtypeStruct((2, rows, W), F32),
        in_specs=[SMEM_SPEC] * 3 + [VMEM_SPEC] * 6,
        out_specs=VMEM_SPEC,
        compiler_params=pltpu.CompilerParams(vmem_limit_bytes=VMEM_BYTES),
        name="add_terms",
    )


def on_device(probe_wave, transmission, kernel_phase, measured, counts, positions, widths):
    groups, tiles = lax.axis_size("cuts"), lax.axis_size("tile")
    group, tile = lax.axis_index("cuts"), lax.axis_index("tile")
    cap = positions.shape[1]
    rows = transmission.shape[2]
    image, pos = transmission[0], positions[0]
    up = [(i, i + 1) for i in range(tiles - 1)]
    down = [(i + 1, i) for i in range(tiles - 1)]

    def to_up(value):
        return lax.ppermute(value, "tile", up)

    def to_down(value):
        return lax.ppermute(value, "tile", down)

    def shift(value, by, keep):
        pairs = [
            (g * tiles + t, (g + by) % groups * tiles + t)
            for g in range(groups)
            for t in range(tiles)
            if keep(g, (g + by) % groups, t % 2)
        ]
        return lax.ppermute(value, ("cuts", "tile"), pairs)

    meta = jnp.stack(
        [group, tile, tile % 2, counts[0], widths[0, 0], widths[0, 1], jnp.int32(tiles)]
    ).astype(jnp.int32)
    pos_left, pos_right = to_up(pos), to_down(pos)
    rims_left, rims_right = cut_rims(cap)(pos_left, pos_right, image)
    from_right, from_left = to_down(rims_left), to_up(rims_right)
    wins = make_windows()(meta, pos, image, from_left, from_right)

    order = jnp.asarray(ORDER)
    exact = lax.Precision.HIGHEST
    phase = jnp.dot(jnp.dot(order, kernel_phase, precision=exact), order.T, precision=exact)
    kern = jnp.stack([jnp.cos(phase), jnp.sin(phase)])
    tab = jnp.asarray(TABLES)
    hot, hot_t = order.astype(BF16), order.T.astype(BF16)

    def shifted(values, keep):
        return [values[0]] + [shift(values[k], k, keep) for k in range(1, 4)]

    all_pairs = lambda src, dst, parity: True
    to_owner = lambda src, dst, parity: dst % 2 == parity
    inner = lambda src, dst, parity: dst != 0
    inner_owned = lambda src, dst, parity: dst != 0 and src % 2 == parity
    owned = lambda src, dst, parity: src % 2 == parity

    got1 = shifted(wins[:4], all_pairs)
    got2 = shifted(wins[4:], to_owner)
    *in1, back1 = forward_slot(0)(meta, pos, probe_wave, measured[0], kern, tab, hot, hot_t, *got1)
    in1 = shifted(in1, inner)
    turned1 = shifted(backward_slot(0)(meta, back1, kern, tab, *got1), all_pairs)
    *in2, back2 = forward_slot(1)(meta, pos, probe_wave, measured[0], kern, tab, hot, hot_t, *got2)
    in2 = shifted(in2, inner_owned)
    turned2 = shifted(backward_slot(1)(meta, back2, kern, tab, *got2), owned)

    adjoint, own1, left1, right1 = slice_terms(0, cap)(
        meta, pos, probe_wave, *turned1, *in1, *wins[:4]
    )
    right1, left1 = to_down(left1), to_up(right1)
    adjoint, own2, left2, right2 = slice_terms(1, cap)(
        meta, pos, probe_wave, adjoint, *turned2, *in2, *wins[4:]
    )
    right2, left2 = to_down(left2), to_up(right2)
    grad = add_terms(cap, rows)(
        pos, pos_left, pos_right, own1, own2, left1, left2, right1, right2
    )
    return adjoint[None, None], grad[None]


def solution(mesh):
    return jax.shard_map(
        on_device,
        mesh=mesh,
        in_specs=(
            P(),
            P("cuts", None, None, "tile"),
            P(),
            P("tile", None, None, None),
            P("tile"),
            P("tile", None, None),
            P("tile", None),
        ),
        out_specs=(P("cuts", "tile", None, None, None, None), P("cuts", None, None, "tile")),
        check_vma=False,
    )
```

```python
import math

import jax
import jax.numpy as jnp
import ml_dtypes
import numpy as np
from jax import lax
from jax.experimental import pallas as pl
from jax.experimental.pallas import tpu as pltpu
from jax.sharding import PartitionSpec as P

RIM = 128
HALF = 128
W = 256
F32 = jnp.float32
BF16 = jnp.bfloat16
VMEM_BYTES = 56 * 1024 * 1024

ANY_SPEC = pl.BlockSpec(memory_space=pl.ANY)
SMEM_SPEC = pl.BlockSpec(memory_space=pltpu.SMEM)
VMEM_SPEC = pl.BlockSpec(memory_space=pltpu.VMEM)


def split_table(table):
    high = table.astype(ml_dtypes.bfloat16)
    low = (table - high.astype(np.float64)).astype(ml_dtypes.bfloat16)
    return high, low


def make_tables():
    freq = np.arange(HALF)[:, None]
    place = np.arange(HALF)[None, :]
    out = []
    for odd in (0, 1):
        angle = 2.0 * math.pi * (((2 * freq + odd) * place) % W) / W
        re, im = np.cos(angle) / math.sqrt(W), -np.sin(angle) / math.sqrt(W)
        real = np.block([[re, -im], [im, re]])
        out += [*split_table(real), *split_table(real.T)]
    return np.stack(out)


def make_order():
    order = np.concatenate([np.arange(0, W, 2), np.arange(1, W, 2)])
    hot = np.zeros((W, W), np.float32)
    hot[np.arange(W), order] = 1.0
    return hot


TABLES = make_tables()
ORDER = make_order()


def dot(first, second):
    return jnp.dot(first, second, preferred_element_type=F32)


def split(value):
    high = value.astype(BF16)
    return high, (value - high.astype(F32)).astype(BF16)


def table_left(tab, at, value):
    high, low = split(value)
    return dot(tab[at], high) + dot(tab[at], low) + dot(tab[at + 1], high)


def table_right(value, tab, at):
    high, low = split(value)
    return dot(high, tab[at]) + dot(low, tab[at]) + dot(high, tab[at + 1])


def to_spectrum(re, im, tab):
    h = HALF
    total = jnp.concatenate([re[:h] + re[h:], im[:h] + im[h:]], 0)
    diff = jnp.concatenate([re[:h] - re[h:], im[:h] - im[h:]], 0)
    even = table_left(tab, 0, total)
    odd = table_left(tab, 4, diff)
    yr = jnp.concatenate([even[:h], odd[:h]], 0)
    yi = jnp.concatenate([even[h:], odd[h:]], 0)
    total = jnp.concatenate([yr[:, :h] + yr[:, h:], yi[:, :h] + yi[:, h:]], 1)
    diff = jnp.concatenate([yr[:, :h] - yr[:, h:], yi[:, :h] - yi[:, h:]], 1)
    return table_right(total, tab, 2), table_right(diff, tab, 6)


def from_spectrum(even, odd, tab):
    h = HALF
    a = table_right(even, tab, 0)
    b = table_right(odd, tab, 4)
    yr = jnp.concatenate([a[:, :h] + b[:, :h], a[:, :h] - b[:, :h]], 1)
    yi = jnp.concatenate([a[:, h:] + b[:, h:], a[:, h:] - b[:, h:]], 1)
    p = table_left(tab, 2, jnp.concatenate([yr[:h], yi[:h]], 0))
    q = table_left(tab, 6, jnp.concatenate([yr[h:], yi[h:]], 0))
    re = jnp.concatenate([p[:h] + q[:h], p[:h] - q[:h]], 0)
    im = jnp.concatenate([p[h:] + q[h:], p[h:] - q[h:]], 0)
    return re, im


def turn(spectrum, cosine, sine):
    h = HALF
    re, im = spectrum[:, :h], spectrum[:, h:]
    return jnp.concatenate([re * cosine - im * sine, re * sine + im * cosine], 1)


def propagate(re, im, kern, tab, sign):
    h = HALF
    even, odd = to_spectrum(re, im, tab)
    cosine, sine = kern[0], sign * kern[1]
    even = turn(even, cosine[:, :h], sine[:, :h])
    odd = turn(odd, cosine[:, h:], sine[:, h:])
    return from_spectrum(even, odd, tab)


def cost(us):
    return pl.CostEstimate(flops=0, transcendentals=0, bytes_accessed=int(us * 3.3e6))


def params():
    return pltpu.CompilerParams(vmem_limit_bytes=VMEM_BYTES)


def row_base(row):
    base = pl.multiple_of((row // 8) * 8, 8)
    extra = pl.multiple_of(jnp.where(base + W < 4096, base + W, base - 8), 8)
    return base, extra, row - base


def rows_below(delta, shape):
    return lax.broadcasted_iota(jnp.int32, shape, len(shape) - 2) < delta


def aligned(cols):
    return pl.ds(pl.multiple_of(cols, HALF), HALF)


def slot_of(owner, second):
    return 4 + owner // 2 if second else owner


def is_owner(owner, second):
    return owner % 2 == lax.axis_index("tile") % 2 if second else owner >= 0


STRIP = jax.ShapeDtypeStruct((2, W, HALF), F32)
FIELD = jax.ShapeDtypeStruct((2, W, W), F32)


class Cut:
    def __init__(self, image, row, cols, out, extra, sems):
        base, more, self.delta = row_base(row)
        self.out, self.extra = out, extra
        cols = aligned(cols)
        self.copies = (
            pltpu.make_async_copy(image.at[:, pl.ds(base, W), cols], out, sems.at[0]),
            pltpu.make_async_copy(image.at[:, pl.ds(more, 8), cols], extra, sems.at[1]),
        )

    def start(self):
        for copy in self.copies:
            copy.start()

    def finish(self):
        for copy in self.copies:
            copy.wait()
        mask = rows_below(self.delta, (2, 8, HALF))
        self.out[:, 0:8, :] = jnp.where(mask, self.extra[...], self.out[:, 0:8, :])


def cut_rims(cap):
    def kernel(pos_left, pos_right, image, *rest):
        outs, (buf, extra, sems, put_sems) = rest[:2], rest[2:]
        cuts, puts = [], []
        for s in range(cap):
            for side, pos in enumerate((pos_left, pos_right)):
                at = 2 * s + side
                cuts.append(
                    Cut(image, pos[s, 0], side * HALF, buf.at[at], extra.at[at], sems.at[at])
                )
                puts.append(pltpu.make_async_copy(buf.at[at], outs[side].at[s], put_sems.at[at]))
        for cut in cuts:
            cut.start()
        for cut, put in zip(cuts, puts):
            cut.finish()
            put.start()
        for put in puts:
            put.wait()

    strips = jax.ShapeDtypeStruct((cap, 2, W, HALF), F32)
    return pl.pallas_call(
        kernel,
        out_shape=(strips, strips),
        in_specs=[SMEM_SPEC, SMEM_SPEC, ANY_SPEC],
        out_specs=(ANY_SPEC, ANY_SPEC),
        scratch_shapes=[
            pltpu.VMEM((2 * cap, 2, W, HALF), F32),
            pltpu.VMEM((2 * cap, 2, 8, HALF), F32),
            pltpu.SemaphoreType.DMA((2 * cap, 2)),
            pltpu.SemaphoreType.DMA((2 * cap,)),
        ],
        compiler_params=params(),
        cost_estimate=cost(4),
        name="cut_rims",
    )


def pure_halves():
    def kernel(pos, image, *rest):
        outs, (extra, sems) = rest[:4], rest[4:]
        group = lax.axis_index("cuts")
        cuts = []
        for k in range(4):
            s = slot_of((group + k) % 4, 0)
            cols = jnp.where(pos[s, 1] > RIM, HALF, 0)
            cuts.append(Cut(image, pos[s, 0], cols, outs[k], extra.at[k], sems.at[k]))
        for cut in cuts:
            cut.start()
        for cut in cuts:
            cut.finish()

    return pl.pallas_call(
        kernel,
        out_shape=(STRIP,) * 4,
        in_specs=[SMEM_SPEC, ANY_SPEC],
        out_specs=(VMEM_SPEC,) * 4,
        scratch_shapes=[
            pltpu.VMEM((4, 2, 8, HALF), F32),
            pltpu.SemaphoreType.DMA((4, 2)),
        ],
        compiler_params=params(),
        cost_estimate=cost(3),
        name="pure_halves",
    )


def mixed_windows():
    def kernel(pos, widths, image, from_left, from_right, *rest):
        outs, bufs, (extra, rim, sems) = rest[:8], rest[8:16], rest[16:]
        group, tile = lax.axis_index("cuts"), lax.axis_index("tile")
        tiles = lax.axis_size("tile")

        def transfers(at, s):
            base, more, _ = row_base(pos[s, 0])
            cols = pl.ds(0, W) if at >= 4 else aligned(jnp.where(pos[s, 1] > RIM, 0, HALF))
            few = extra.at[at] if at >= 4 else extra.at[at, :, :, pl.ds(0, HALF)]
            return (
                pltpu.make_async_copy(image.at[:, pl.ds(base, W), cols], bufs[at], sems.at[at, 0]),
                pltpu.make_async_copy(image.at[:, pl.ds(more, 8), cols], few, sems.at[at, 1]),
            )

        def rim_copy(at, s, source):
            return pltpu.make_async_copy(source.at[s], rim.at[at], sems.at[at, 2])

        def put(at, s):
            return pltpu.make_async_copy(bufs[at], outs[at], sems.at[at, 3])

        def each(job):
            for at in range(8):
                second, k = divmod(at, 4)
                owner = (group + k) % 4
                pl.when(is_owner(owner, second))(
                    lambda at=at, owner=owner, second=second: job(at, slot_of(owner, second))
                )

        def begin(at, s):
            for copy in transfers(at, s):
                copy.start()

            @pl.when(pos[s, 1] > RIM)
            def _():
                rim_copy(at, s, from_right).start()

            @pl.when(pos[s, 1] <= RIM)
            def _():
                rim_copy(at, s, from_left).start()

        def work(at, s):
            for copy in transfers(at, s):
                copy.wait()
            edge = pos[s, 1] - RIM
            out = bufs[at]
            width = out.shape[-1]
            mask = rows_below(pos[s, 0] % 8, (2, 8, width))
            out[:, 0:8, :] = jnp.where(mask, extra[at, :, :, :width], out[:, 0:8, :])
            lane = lax.broadcasted_iota(jnp.int32, (W, HALF), 1)
            low, high = slice(0, HALF), slice(width - HALF, width)

            @pl.when(edge > 0)
            def _():
                rim_copy(at, s, from_right).wait()
                kept = (lane < widths[0, 1]) & (tile < tiles - 1)
                for part in range(2):
                    value = jnp.where(kept, rim[at, part], 1.0 - part)
                    out[part, :, low] = jnp.where(lane < edge, value, out[part, :, low])

            @pl.when(edge <= 0)
            def _():
                rim_copy(at, s, from_left).wait()
                kept = (lane >= HALF - widths[0, 0]) & (tile > 0)
                for part in range(2):
                    value = jnp.where(kept, rim[at, part], 1.0 - part)
                    out[part, :, high] = jnp.where(lane >= HALF + edge, value, out[part, :, high])

            put(at, s).start()

        each(begin)
        each(work)
        each(lambda at, s: put(at, s).wait())

    return pl.pallas_call(
        kernel,
        out_shape=(STRIP,) * 4 + (FIELD,) * 4,
        in_specs=[SMEM_SPEC, SMEM_SPEC, ANY_SPEC, ANY_SPEC, ANY_SPEC],
        out_specs=(ANY_SPEC,) * 8,
        scratch_shapes=[pltpu.VMEM((2, W, HALF), F32)] * 4
        + [pltpu.VMEM((2, W, W), F32)] * 4
        + [
            pltpu.VMEM((8, 2, 8, W), F32),
            pltpu.VMEM((8, 2, W, HALF), F32),
            pltpu.SemaphoreType.DMA((8, 4)),
        ],
        compiler_params=params(),
        cost_estimate=cost(5),
        name="mixed_windows",
    )


class Windows:
    def __init__(self, refs, buf, right, sems):
        self.refs, self.buf, self.sems = refs, buf, sems
        self.at = jnp.where(right, HALF, 0)

    def copies(self, k, n):
        out = self.buf.at[n]
        if len(self.refs) == 4:
            return [pltpu.make_async_copy(self.refs[k], out, self.sems.at[n, 0])]
        pure, mixed = self.refs[k], self.refs[4 + k]
        return [
            pltpu.make_async_copy(pure, out.at[:, :, aligned(self.at)], self.sems.at[n, 0]),
            pltpu.make_async_copy(mixed, out.at[:, :, aligned(HALF - self.at)], self.sems.at[n, 1]),
        ]

    def start(self):
        for k in range(4):
            for copy in self.copies(k, (lax.axis_index("cuts") - k) % 4):
                copy.start()

    def wait(self, n):
        for copy in self.copies(0, n):
            copy.wait()


class Loads:
    def __init__(self, refs, bufs, sems):
        self.copies = [
            pltpu.make_async_copy(ref, buf, sems.at[at])
            for at, (ref, buf) in enumerate(zip(refs, bufs))
        ]
        for copy in self.copies:
            copy.start()

    def wait(self, *which):
        for at in which:
            self.copies[at].wait()


CONSTANTS = [
    pltpu.VMEM((2, W, W), F32),
    pltpu.VMEM((8, W, W), BF16),
    pltpu.VMEM((2, W, W), F32),
    pltpu.VMEM((W, W), BF16),
    pltpu.VMEM((W, W), BF16),
    pltpu.SemaphoreType.DMA((5,)),
]


def place_probe(probe, row, col, scale, out):
    for part in range(2):
        rolled = pltpu.roll(probe[part], (col - RIM) % W, 1)
        out[part] = pltpu.roll(rolled, row % 8, 0) * scale


def forward_steps(wins, in_buf, kern, tab):
    def step(n, carry):
        wins.wait(n)
        re, im = in_buf[n, 0], in_buf[n, 1]
        wr, wi = wins.buf[n, 0], wins.buf[n, 1]
        re, im = wr * re - wi * im, wr * im + wi * re
        re, im = propagate(re, im, kern, tab, 1.0)
        in_buf[n + 1, 0] = re
        in_buf[n + 1, 1] = im
        return carry

    lax.fori_loop(0, 4, step, 0)


def far_step(in_buf, seen, order, order_t, tab, back):
    half_seen = dot(order[...], seen[...]).astype(BF16)
    target = dot(half_seen, order_t[...])
    spectra = to_spectrum(in_buf[4, 0], in_buf[4, 1], tab)
    chis = []
    for odd in range(2):
        re, im = spectra[odd][:, :HALF], spectra[odd][:, HALF:]
        excess = re * re + im * im - target[:, odd * HALF : (odd + 1) * HALF]
        chis.append(jnp.concatenate([re * excess, im * excess], 1))
    re, im = from_spectrum(chis[0], chis[1], tab)
    back[0] = re
    back[1] = im


def backward_steps(wins, turned_buf, back, kern, tab, store):
    def step(at, carry):
        n = 3 - at
        re, im = propagate(back[0], back[1], kern, tab, -1.0)
        turned_buf[n, 0] = re
        turned_buf[n, 1] = im
        for k in range(4):
            pl.when((lax.axis_index("cuts") + k) % 4 == n)(lambda k=k: store(k, n).start())
        wr, wi = wins.buf[n, 0], wins.buf[n, 1]
        back[0] = wr * re + wi * im
        back[1] = wr * im - wi * re
        return carry

    lax.fori_loop(0, 4, step, 0)


def forward_first():
    def kernel(pos, counts, probe, measured, kern, tab, order, order_t, *rest):
        refs, inputs, back = rest[:8], rest[8:12], rest[12]
        win_buf, in_buf, seen, load_sems, sems, *held = rest[13:]
        group = lax.axis_index("cuts")
        s = slot_of(group, 0)
        *bufs, const_sems = held
        consts = Loads((probe, tab, kern, order, order_t), bufs, const_sems)
        probe, tab, kern, order, order_t = bufs
        wins = Windows(refs, win_buf, pos[s, 1] > RIM, load_sems)
        wins.start()
        seeing = pltpu.make_async_copy(measured.at[s], seen, sems.at[4])
        seeing.start()
        consts.wait(0)
        place_probe(probe, pos[s, 0], pos[s, 1], jnp.where(s < counts[0], 1.0, 0.0), in_buf.at[0])
        consts.wait(1, 2)
        forward_steps(wins, in_buf, kern, tab)
        stores = [
            pltpu.make_async_copy(in_buf.at[(group + k) % 4], inputs[k], sems.at[k])
            for k in range(4)
        ]
        for copy in stores:
            copy.start()
        seeing.wait()
        consts.wait(3, 4)
        far_step(in_buf, seen, order, order_t, tab, back)
        for copy in stores:
            copy.wait()

    return pl.pallas_call(
        kernel,
        out_shape=(FIELD,) * 5,
        in_specs=[SMEM_SPEC, SMEM_SPEC] + [ANY_SPEC] * 14,
        out_specs=(ANY_SPEC,) * 4 + (VMEM_SPEC,),
        scratch_shapes=[
            pltpu.VMEM((4, 2, W, W), F32),
            pltpu.VMEM((5, 2, W, W), F32),
            pltpu.VMEM((W, W), BF16),
            pltpu.SemaphoreType.DMA((4, 2)),
            pltpu.SemaphoreType.DMA((5,)),
            *CONSTANTS,
        ],
        compiler_params=params(),
        cost_estimate=cost(9),
        name="forward_first",
    )


def backward_first():
    def kernel(pos, back, kern, tab, *rest):
        refs, turned = rest[:8], rest[8:12]
        win_buf, turned_buf, back_buf, load_sems, sems, *held = rest[12:]
        s = slot_of(lax.axis_index("cuts"), 0)
        *bufs, const_sems = held
        consts = Loads((back, tab, kern), (back_buf, *bufs), const_sems)
        tab, kern = bufs
        wins = Windows(refs, win_buf, pos[s, 1] > RIM, load_sems)
        wins.start()
        consts.wait(0, 1, 2)


        def store(k, n):
            return pltpu.make_async_copy(turned_buf.at[n], turned[k], sems.at[k])

        for n in range(4):
            wins.wait(n)
        backward_steps(wins, turned_buf, back_buf, kern, tab, store)
        for k in range(4):
            store(k, 0).wait()

    return pl.pallas_call(
        kernel,
        out_shape=(FIELD,) * 4,
        in_specs=[SMEM_SPEC] + [ANY_SPEC] * 11,
        out_specs=(ANY_SPEC,) * 4,
        scratch_shapes=[
            pltpu.VMEM((4, 2, W, W), F32),
            pltpu.VMEM((4, 2, W, W), F32),
            pltpu.VMEM((2, W, W), F32),
            pltpu.SemaphoreType.DMA((4, 2)),
            pltpu.SemaphoreType.DMA((4,)),
            pltpu.VMEM((8, W, W), BF16),
            pltpu.VMEM((2, W, W), F32),
            pltpu.SemaphoreType.DMA((3,)),
        ],
        compiler_params=params(),
        cost_estimate=cost(7),
        name="backward_first",
    )


def both_ways(second):
    count = 4 if second else 8

    def kernel(pos, counts, probe, measured, kern, tab, order, order_t, *rest):
        refs, outs = rest[:count], rest[count : count + 4]
        win_buf, in_buf, turned_buf, back_buf, seen, load_sems, sems, *held = rest[count + 4 :]
        group = lax.axis_index("cuts")
        s = slot_of(group, second)

        def store(k, n):
            return pltpu.make_async_copy(turned_buf.at[n], outs[k].at[1], sems.at[4 + k])

        @pl.when(is_owner(group, second))
        def _():
            *bufs, const_sems = held
            consts = Loads((probe, tab, kern, order, order_t), bufs, const_sems)
            probe_buf, tab_buf, kern_buf, order_buf, order_t_buf = bufs
            wins = Windows(refs, win_buf, pos[s, 1] > RIM, load_sems)
            wins.start()
            seeing = pltpu.make_async_copy(measured.at[s], seen, sems.at[8])
            seeing.start()
            scale = jnp.where(s < counts[0], 1.0, 0.0)
            consts.wait(0)
            place_probe(probe_buf, pos[s, 0], pos[s, 1], scale, in_buf.at[0])
            consts.wait(1, 2)
            forward_steps(wins, in_buf, kern_buf, tab_buf)
            stores = [
                pltpu.make_async_copy(in_buf.at[(group + k) % 4], outs[k].at[0], sems.at[k])
                for k in range(4)
            ]
            for copy in stores:
                copy.start()
            seeing.wait()
            consts.wait(3, 4)
            far_step(in_buf, seen, order_buf, order_t_buf, tab_buf, back_buf)
            backward_steps(wins, turned_buf, back_buf, kern_buf, tab_buf, store)
            for copy in stores:
                copy.wait()
            for k in range(4):
                store(k, 0).wait()

    pair = jax.ShapeDtypeStruct((2, 2, W, W), F32)
    return pl.pallas_call(
        kernel,
        out_shape=(pair,) * 4,
        in_specs=[SMEM_SPEC, SMEM_SPEC] + [ANY_SPEC] * (6 + count),
        out_specs=(ANY_SPEC,) * 4,
        scratch_shapes=[
            pltpu.VMEM((4, 2, W, W), F32),
            pltpu.VMEM((5, 2, W, W), F32),
            pltpu.VMEM((4, 2, W, W), F32),
            pltpu.VMEM((2, W, W), F32),
            pltpu.VMEM((W, W), BF16),
            pltpu.SemaphoreType.DMA((4, 2)),
            pltpu.SemaphoreType.DMA((9,)),
            *CONSTANTS,
        ],
        compiler_params=params(),
        cost_estimate=cost(14),
        name="both_second" if second else "both_first",
    )


def each_owner(second, job):
    for j in range(4):
        owner = (lax.axis_index("cuts") - j) % 4
        pl.when(is_owner(owner, second))(lambda j=j, owner=owner: job(j, slot_of(owner, second)))


def adjoint_of(t_buf, w_buf, pos, s, out):
    re, im = t_buf[0], t_buf[1]
    wr, wi = w_buf[0], w_buf[1]
    for part, value in enumerate((wr * re + wi * im, wr * im - wi * re)):
        rolled = pltpu.roll(value, (W + RIM - pos[s, 1]) % W, 1)
        out[part] = pltpu.roll(rolled, (W - pos[s, 0] % 8) % W, 0)


def conj_terms(i_buf, t_buf, half):
    ir, ii = i_buf[0, :, half], i_buf[1, :, half]
    re, im = t_buf[0, :, half], t_buf[1, :, half]
    return ir * re + ii * im, ir * im - ii * re


LOW, HIGH = slice(0, HALF), slice(HALF, W)


def lanes():
    return lax.broadcasted_iota(jnp.int32, (W, HALF), 1)


def rim_terms(i_buf, t_buf, edge, widths, to_left, to_right):
    tile, tiles = lax.axis_index("tile"), lax.axis_size("tile")
    lane = lanes()
    sent_left = (lane >= HALF + edge) & (lane >= HALF - widths[0, 0]) & (tile > 0)
    sent_right = (lane < edge) & (lane < widths[0, 1]) & (tile < tiles - 1)

    @pl.when(edge > 0)
    def _():
        for part, value in enumerate(conj_terms(i_buf, t_buf, LOW)):
            to_right[part] = jnp.where(sent_right, value, 0.0)
            to_left[part] = jnp.zeros_like(value)

    @pl.when(edge <= 0)
    def _():
        for part, value in enumerate(conj_terms(i_buf, t_buf, HIGH)):
            to_left[part] = jnp.where(sent_left, value, 0.0)
            to_right[part] = jnp.zeros_like(value)


def own_terms(i_buf, t_buf, edge):
    lane = lanes()
    low = [jnp.where(lane < edge, 0.0, value) for value in conj_terms(i_buf, t_buf, LOW)]
    high = [jnp.where(lane >= HALF + edge, 0.0, value) for value in conj_terms(i_buf, t_buf, HIGH)]
    return low, high


def terms_first(cap):
    def kernel(pos, counts, widths, probe, *rest):
        inputs, turned, pure, mixed = rest[:4], rest[4:8], rest[8:12], rest[12:16]
        adjoint, own, to_left, to_right = rest[16:20]
        buf, w_buf, a_buf, sems = rest[20:]

        def loads(j, s):
            k = (4 - j) % 4
            at = jnp.where(pos[s, 1] > RIM, HALF, 0)
            out = w_buf.at[j]
            return (
                pltpu.make_async_copy(inputs[j], buf.at[j, 0], sems.at[j, 0]),
                pltpu.make_async_copy(turned[j], buf.at[j, 1], sems.at[j, 1]),
                pltpu.make_async_copy(pure[k], out.at[:, :, aligned(at)], sems.at[j, 2]),
                pltpu.make_async_copy(mixed[k], out.at[:, :, aligned(HALF - at)], sems.at[j, 3]),
            )

        def store(j, s):
            return pltpu.make_async_copy(a_buf.at[j], adjoint.at[s], sems.at[j, 4])

        def begin(j, s):
            for copy in loads(j, s):
                copy.start()

        def work(j, s):
            for copy in loads(j, s):
                copy.wait()
            edge = pos[s, 1] - RIM

            @pl.when(lax.axis_index("cuts") == 0)
            def _():
                scale = jnp.where(s < counts[0], 1.0, 0.0)
                place_probe(probe, pos[s, 0], pos[s, 1], scale, buf.at[j, 0])

            ins, outs = buf.at[j, 0], buf.at[j, 1]
            rim_terms(ins, outs, edge, widths, to_left.at[s], to_right.at[s])
            for half, values in zip((LOW, HIGH), own_terms(ins, outs, edge)):
                for part, value in enumerate(values):
                    own[s, part, :, half] = value
            adjoint_of(outs, w_buf.at[j], pos, s, a_buf.at[j])
            store(j, s).start()

        each_owner(0, begin)
        each_owner(0, work)
        each_owner(0, lambda j, s: store(j, s).wait())

    strips = jax.ShapeDtypeStruct((4, 2, W, HALF), F32)
    return pl.pallas_call(
        kernel,
        out_shape=(
            jax.ShapeDtypeStruct((cap, 2, W, W), F32),
            jax.ShapeDtypeStruct((4, 2, W, W), F32),
            strips,
            strips,
        ),
        in_specs=[SMEM_SPEC] * 3 + [VMEM_SPEC] + [ANY_SPEC] * 16,
        out_specs=(ANY_SPEC, VMEM_SPEC, VMEM_SPEC, VMEM_SPEC),
        scratch_shapes=[
            pltpu.VMEM((4, 2, 2, W, W), F32),
            pltpu.VMEM((4, 2, W, W), F32),
            pltpu.VMEM((4, 2, W, W), F32),
            pltpu.SemaphoreType.DMA((4, 5)),
        ],
        compiler_params=params(),
        cost_estimate=cost(7),
        name="terms_first",
    )


def rims_second(count):
    def kernel(pos, counts, widths, probe, *rest):
        pairs, (to_left, to_right), (buf, sems) = rest[:4], rest[4:6], rest[6:]

        def load(j):
            return pltpu.make_async_copy(pairs[j], buf.at[j], sems.at[j])

        def work(j, s):
            load(j).wait()

            @pl.when(lax.axis_index("cuts") == 0)
            def _():
                scale = jnp.where(s < counts[0], 1.0, 0.0)
                place_probe(probe, pos[s, 0], pos[s, 1], scale, buf.at[j, 0])

            edge = pos[s, 1] - RIM
            at = s - 4
            rim_terms(buf.at[j, 0], buf.at[j, 1], edge, widths, to_left.at[at], to_right.at[at])

        each_owner(1, lambda j, s: load(j).start())
        each_owner(1, work)

    strips = jax.ShapeDtypeStruct((count, 2, W, HALF), F32)
    return pl.pallas_call(
        kernel,
        out_shape=(strips, strips),
        in_specs=[SMEM_SPEC] * 3 + [VMEM_SPEC] + [ANY_SPEC] * 4,
        out_specs=(VMEM_SPEC, VMEM_SPEC),
        scratch_shapes=[pltpu.VMEM((4, 2, 2, W, W), F32), pltpu.SemaphoreType.DMA((4,))],
        compiler_params=params(),
        cost_estimate=cost(3),
        name="rims_second",
    )


class AddInto:
    def __init__(self, grad, row, cols, buf, more_buf, sems):
        base, more, self.delta = row_base(row)
        self.buf, self.more_buf = buf, more_buf
        self.pairs = (
            (grad.at[:, pl.ds(base, W), cols], buf),
            (grad.at[:, pl.ds(more, 8), cols], more_buf),
        )
        self.sems = sems

    def copies(self, inward):
        return [
            pltpu.make_async_copy(
                pair[0 if inward else 1], pair[1 if inward else 0], self.sems.at[at]
            )
            for at, pair in enumerate(self.pairs)
        ]

    def start(self, inward):
        for copy in self.copies(inward):
            copy.start()

    def wait(self, inward):
        for copy in self.copies(inward):
            copy.wait()

    def add(self, part, half, value):
        below = rows_below(self.delta, value.shape)
        self.buf[part, :, half] += jnp.where(below, 0.0, value)
        few = rows_below(self.delta, value[:8].shape)
        self.more_buf[part, :, half] += jnp.where(few, value[:8], 0.0)


def add_rows(out, row, value, cols):
    base, more, delta = row_base(row)
    width = value[0].shape[-1]
    below = rows_below(delta, (W, width))
    few = rows_below(delta, (8, width))
    for part in range(2):
        out[part, pl.ds(base, W), cols] += jnp.where(below, 0.0, value[part])
        out[part, pl.ds(more, 8), cols] += jnp.where(few, value[part][:8], 0.0)


def finish(cap, rows):
    def kernel(pos, pos_left, pos_right, counts, probe, own, left, right, adjoint_in, *rest):
        pairs, full, (adjoint, grad) = rest[:4], rest[4:8], rest[8:10]
        buf, w_buf, a_buf, sems = rest[10:]

        def loads(j):
            return (
                pltpu.make_async_copy(pairs[j], buf.at[j], sems.at[j, 0]),
                pltpu.make_async_copy(full[(4 - j) % 4], w_buf.at[j], sems.at[j, 1]),
            )

        def store(j, s):
            return pltpu.make_async_copy(a_buf.at[j], adjoint.at[s], sems.at[j, 2])

        def begin(j, s):
            for copy in loads(j):
                copy.start()

        def work(j, s):
            for copy in loads(j):
                copy.wait()

            @pl.when(lax.axis_index("cuts") == 0)
            def _():
                scale = jnp.where(s < counts[0], 1.0, 0.0)
                place_probe(probe, pos[s, 0], pos[s, 1], scale, buf.at[j, 0])

            adjoint_of(buf.at[j, 1], w_buf.at[j], pos, s, a_buf.at[j])
            store(j, s).start()
            terms = own_terms(buf.at[j, 0], buf.at[j, 1], pos[s, 1] - RIM)
            for half, values in zip((LOW, HIGH), terms):
                add_rows(grad, pos[s, 0], values, half)

        each_owner(1, begin)
        grad[...] = jnp.zeros_like(grad)
        for s in range(4):
            add_rows(grad, pos[s, 0], own[s], slice(0, W))
            add_rows(grad, pos_left[s, 0], left[s], LOW)
            add_rows(grad, pos_right[s, 0], right[s], HIGH)
        each_owner(1, work)
        each_owner(1, lambda j, s: store(j, s).wait())

    return pl.pallas_call(
        kernel,
        out_shape=(
            jax.ShapeDtypeStruct((cap, 2, W, W), F32),
            jax.ShapeDtypeStruct((2, rows, W), F32),
        ),
        in_specs=[SMEM_SPEC] * 4 + [VMEM_SPEC] * 4 + [ANY_SPEC] * 9,
        out_specs=(ANY_SPEC, VMEM_SPEC),
        scratch_shapes=[
            pltpu.VMEM((4, 2, 2, W, W), F32),
            pltpu.VMEM((4, 2, W, W), F32),
            pltpu.VMEM((4, 2, W, W), F32),
            pltpu.SemaphoreType.DMA((4, 3)),
        ],
        input_output_aliases={8: 0},
        compiler_params=params(),
        cost_estimate=cost(9),
        name="finish",
    )


def add_rims(count, rows):
    def kernel(pos_left, pos_right, grad_in, left, right, grad, buf, more_buf, sems):
        for s in range(count):
            adders = [
                AddInto(
                    grad,
                    pos[4 + s, 0],
                    pl.ds(side * HALF, HALF),
                    buf.at[side],
                    more_buf.at[side],
                    sems.at[side],
                )
                for side, pos in enumerate((pos_left, pos_right))
            ]
            for add in adders:
                add.start(True)
            for add, values in zip(adders, (left, right)):
                add.wait(True)
                for part in range(2):
                    add.add(part, LOW, values[s, part])
                add.start(False)
            for add in adders:
                add.wait(False)

    return pl.pallas_call(
        kernel,
        out_shape=jax.ShapeDtypeStruct((2, rows, W), F32),
        in_specs=[SMEM_SPEC] * 2 + [ANY_SPEC] + [VMEM_SPEC] * 2,
        out_specs=ANY_SPEC,
        scratch_shapes=[
            pltpu.VMEM((2, 2, W, HALF), F32),
            pltpu.VMEM((2, 2, 8, HALF), F32),
            pltpu.SemaphoreType.DMA((2, 2)),
        ],
        input_output_aliases={2: 0},
        compiler_params=params(),
        cost_estimate=cost(4),
        name="add_rims",
    )


def after(value, *others):
    return lax.optimization_barrier((value, *others))[0]


def on_device(probe_wave, transmission, kernel_phase, measured, counts, positions, widths):
    groups, tiles = lax.axis_size("cuts"), lax.axis_size("tile")
    cap = positions.shape[1]
    rows = transmission.shape[2]
    image, pos = transmission[0], positions[0]
    up = [(i, i + 1) for i in range(tiles - 1)]
    down = [(i + 1, i) for i in range(tiles - 1)]

    def to_up(value):
        return lax.ppermute(value, "tile", up)

    def to_down(value):
        return lax.ppermute(value, "tile", down)

    def shift(value, by, keep):
        pairs = [
            (g * tiles + t, (g + by) % groups * tiles + t)
            for g in range(groups)
            for t in range(tiles)
            if keep(g, (g + by) % groups, t % 2)
        ]
        return lax.ppermute(value, ("cuts", "tile"), pairs)

    def shifted(values, keep):
        moved = {k: shift(values[k], k, keep) for k in (1, 3, 2)}
        return [values[0], moved[1], moved[2], moved[3]]

    every = lambda src, dst, parity: True
    to_owner = lambda src, dst, parity: dst % 2 == parity
    inner = lambda src, dst, parity: dst != 0
    owned = lambda src, dst, parity: src % 2 == parity

    order = jnp.asarray(ORDER)
    exact = lax.Precision.HIGHEST
    phase = jnp.dot(jnp.dot(order, kernel_phase, precision=exact), order.T, precision=exact)
    kern = jnp.stack([jnp.cos(phase), jnp.sin(phase)])
    tab = jnp.asarray(TABLES)
    hot, hot_t = order.astype(BF16), order.T.astype(BF16)

    pos_left, pos_right = to_up(pos), to_down(pos)
    pure1 = pure_halves()(pos, image)
    got_pure1 = shifted(pure1, every)
    edge_left, edge_right = cut_rims(cap)(pos_left, pos_right, image)
    rim_right, rim_left = to_down(edge_left), to_up(edge_right)
    rim_left = after(rim_left, kern, *got_pure1[1:])

    made = mixed_windows()(pos, widths, image, rim_left, rim_right)
    mixed1, full2 = made[:4], made[4:]
    got_mixed1 = shifted(mixed1, every)
    got_full2 = shifted([after(value, *got_mixed1[1:]) for value in full2], to_owner)

    wide = (probe_wave, measured[0], kern, tab, hot, hot_t)
    *in1, back1 = forward_first()(pos, counts, *wide, *got_pure1, *got_mixed1)
    got_in1 = shifted(in1, inner)
    back1 = after(back1, *got_full2[1:])
    turned1 = backward_first()(pos, back1, kern, tab, *got_pure1, *got_mixed1)
    got_turned1 = shifted(turned1, every)
    got_full2[0] = after(got_full2[0], turned1[1], got_in1[1])
    pairs2 = both_ways(1)(pos, counts, *wide, *got_full2)
    got_pairs2 = shifted(pairs2, owned)

    adjoint, own1, left1, right1 = terms_first(cap)(
        pos, counts, widths, probe_wave, *got_in1, *got_turned1, *pure1, *mixed1
    )
    right1, left1 = to_down(left1), to_up(right1)
    left2, right2 = rims_second(cap - 4)(pos, counts, widths, probe_wave, *got_pairs2)
    own1 = after(own1, left2)
    right2, left2 = to_down(left2), to_up(right2)
    adjoint, grad = finish(cap, rows)(
        pos, pos_left, pos_right, counts, probe_wave, own1, left1, right1, adjoint,
        *got_pairs2, *full2
    )
    grad = add_rims(cap - 4, rows)(pos_left, pos_right, grad, left2, right2)
    return adjoint[None, None], grad[None]


def solution(mesh):
    return jax.shard_map(
        on_device,
        mesh=mesh,
        in_specs=(
            P(),
            P("cuts", None, None, "tile"),
            P(),
            P("tile", None, None, None),
            P("tile"),
            P("tile", None, None),
            P("tile", None),
        ),
        out_specs=(P("cuts", "tile", None, None, None, None), P("cuts", None, None, "tile")),
        check_vma=False,
    )
```

```python
import math

import jax
import jax.numpy as jnp
import ml_dtypes
import numpy as np
from jax import lax
from jax.experimental import pallas as pl
from jax.experimental.pallas import tpu as pltpu
from jax.sharding import PartitionSpec as P

RIM = 128
HALF = 128
W = 256
F32 = jnp.float32
BF16 = jnp.bfloat16
VMEM_BYTES = 56 * 1024 * 1024

ANY_SPEC = pl.BlockSpec(memory_space=pl.ANY)
SMEM_SPEC = pl.BlockSpec(memory_space=pltpu.SMEM)
VMEM_SPEC = pl.BlockSpec(memory_space=pltpu.VMEM)


def split_table(table):
    high = table.astype(ml_dtypes.bfloat16)
    low = (table - high.astype(np.float64)).astype(ml_dtypes.bfloat16)
    return high, low


def make_tables():
    freq = np.arange(HALF)[:, None]
    place = np.arange(HALF)[None, :]
    out = []
    for odd in (0, 1):
        angle = 2.0 * math.pi * (((2 * freq + odd) * place) % W) / W
        re, im = np.cos(angle) / math.sqrt(W), -np.sin(angle) / math.sqrt(W)
        real = np.block([[re, -im], [im, re]])
        out += [*split_table(real), *split_table(real.T)]
    return np.stack(out)


def make_order():
    order = np.concatenate([np.arange(0, W, 2), np.arange(1, W, 2)])
    hot = np.zeros((W, W), np.float32)
    hot[np.arange(W), order] = 1.0
    return hot


TABLES = make_tables()
ORDER = make_order()


def dot(first, second):
    return jnp.dot(first, second, preferred_element_type=F32)


def split(value):
    high = value.astype(BF16)
    return high, (value - high.astype(F32)).astype(BF16)


def table_left(tab, at, value):
    high, low = split(value)
    return dot(tab[at], high) + dot(tab[at], low) + dot(tab[at + 1], high)


def table_right(value, tab, at):
    high, low = split(value)
    return dot(high, tab[at]) + dot(low, tab[at]) + dot(high, tab[at + 1])


def to_spectrum(re, im, tab):
    h = HALF
    total = jnp.concatenate([re[:h] + re[h:], im[:h] + im[h:]], 0)
    diff = jnp.concatenate([re[:h] - re[h:], im[:h] - im[h:]], 0)
    even = table_left(tab, 0, total)
    odd = table_left(tab, 4, diff)
    yr = jnp.concatenate([even[:h], odd[:h]], 0)
    yi = jnp.concatenate([even[h:], odd[h:]], 0)
    total = jnp.concatenate([yr[:, :h] + yr[:, h:], yi[:, :h] + yi[:, h:]], 1)
    diff = jnp.concatenate([yr[:, :h] - yr[:, h:], yi[:, :h] - yi[:, h:]], 1)
    return table_right(total, tab, 2), table_right(diff, tab, 6)


def from_spectrum(even, odd, tab):
    h = HALF
    a = table_right(even, tab, 0)
    b = table_right(odd, tab, 4)
    yr = jnp.concatenate([a[:, :h] + b[:, :h], a[:, :h] - b[:, :h]], 1)
    yi = jnp.concatenate([a[:, h:] + b[:, h:], a[:, h:] - b[:, h:]], 1)
    p = table_left(tab, 2, jnp.concatenate([yr[:h], yi[:h]], 0))
    q = table_left(tab, 6, jnp.concatenate([yr[h:], yi[h:]], 0))
    re = jnp.concatenate([p[:h] + q[:h], p[:h] - q[:h]], 0)
    im = jnp.concatenate([p[h:] + q[h:], p[h:] - q[h:]], 0)
    return re, im


def turn(spectrum, cosine, sine):
    h = HALF
    re, im = spectrum[:, :h], spectrum[:, h:]
    return jnp.concatenate([re * cosine - im * sine, re * sine + im * cosine], 1)


def propagate(re, im, kern, tab, sign):
    h = HALF
    even, odd = to_spectrum(re, im, tab)
    cosine, sine = kern[0], sign * kern[1]
    even = turn(even, cosine[:, :h], sine[:, :h])
    odd = turn(odd, cosine[:, h:], sine[:, h:])
    return from_spectrum(even, odd, tab)


def cost(us):
    return pl.CostEstimate(flops=0, transcendentals=0, bytes_accessed=int(us * 3.3e6))


def params():
    return pltpu.CompilerParams(vmem_limit_bytes=VMEM_BYTES)


def row_base(row):
    base = pl.multiple_of((row // 8) * 8, 8)
    extra = pl.multiple_of(jnp.where(base + W < 4096, base + W, base - 8), 8)
    return base, extra, row - base


def rows_below(delta, shape):
    return lax.broadcasted_iota(jnp.int32, shape, len(shape) - 2) < delta


def aligned(cols):
    return pl.ds(pl.multiple_of(cols, HALF), HALF)


def slot_of(owner, second):
    return 4 + owner // 2 if second else owner


def is_owner(owner, second):
    return owner % 2 == lax.axis_index("tile") % 2 if second else owner >= 0


STRIP = jax.ShapeDtypeStruct((2, W, HALF), F32)
FIELD = jax.ShapeDtypeStruct((2, W, W), F32)


class Cut:
    def __init__(self, image, row, cols, out, extra, sems):
        base, more, self.delta = row_base(row)
        self.out, self.extra = out, extra
        cols = aligned(cols)
        self.copies = (
            pltpu.make_async_copy(image.at[:, pl.ds(base, W), cols], out, sems.at[0]),
            pltpu.make_async_copy(image.at[:, pl.ds(more, 8), cols], extra, sems.at[1]),
        )

    def start(self):
        for copy in self.copies:
            copy.start()

    def finish(self):
        for copy in self.copies:
            copy.wait()
        mask = rows_below(self.delta, (2, 8, HALF))
        self.out[:, 0:8, :] = jnp.where(mask, self.extra[...], self.out[:, 0:8, :])


def cut_rims(cap):
    def kernel(pos_left, pos_right, image, *rest):
        outs, (buf, extra, sems, put_sems) = rest[:2], rest[2:]
        cuts, puts = [], []
        for s in range(cap):
            for side, pos in enumerate((pos_left, pos_right)):
                at = 2 * s + side
                cuts.append(
                    Cut(image, pos[s, 0], side * HALF, buf.at[at], extra.at[at], sems.at[at])
                )
                puts.append(pltpu.make_async_copy(buf.at[at], outs[side].at[s], put_sems.at[at]))
        for cut in cuts:
            cut.start()
        for cut, put in zip(cuts, puts):
            cut.finish()
            put.start()
        for put in puts:
            put.wait()

    strips = jax.ShapeDtypeStruct((cap, 2, W, HALF), F32)
    return pl.pallas_call(
        kernel,
        out_shape=(strips, strips),
        in_specs=[SMEM_SPEC, SMEM_SPEC, ANY_SPEC],
        out_specs=(ANY_SPEC, ANY_SPEC),
        scratch_shapes=[
            pltpu.VMEM((2 * cap, 2, W, HALF), F32),
            pltpu.VMEM((2 * cap, 2, 8, HALF), F32),
            pltpu.SemaphoreType.DMA((2 * cap, 2)),
            pltpu.SemaphoreType.DMA((2 * cap,)),
        ],
        compiler_params=params(),
        cost_estimate=cost(4),
        name="cut_rims",
    )


def pure_halves():
    def kernel(pos, image, *rest):
        outs, (extra, sems) = rest[:4], rest[4:]
        group = lax.axis_index("cuts")
        cuts = []
        for k in range(4):
            s = slot_of((group + k) % 4, 0)
            cols = jnp.where(pos[s, 1] > RIM, HALF, 0)
            cuts.append(Cut(image, pos[s, 0], cols, outs[k], extra.at[k], sems.at[k]))
        for cut in cuts:
            cut.start()
        for cut in cuts:
            cut.finish()

    return pl.pallas_call(
        kernel,
        out_shape=(STRIP,) * 4,
        in_specs=[SMEM_SPEC, ANY_SPEC],
        out_specs=(VMEM_SPEC,) * 4,
        scratch_shapes=[
            pltpu.VMEM((4, 2, 8, HALF), F32),
            pltpu.SemaphoreType.DMA((4, 2)),
        ],
        compiler_params=params(),
        cost_estimate=cost(3),
        name="pure_halves",
    )


def mixed_windows():
    def kernel(pos, widths, image, from_left, from_right, *rest):
        outs, bufs, (extra, rim, sems) = rest[:8], rest[8:16], rest[16:]
        group, tile = lax.axis_index("cuts"), lax.axis_index("tile")
        tiles = lax.axis_size("tile")

        def transfers(at, s):
            base, more, _ = row_base(pos[s, 0])
            cols = pl.ds(0, W) if at >= 4 else aligned(jnp.where(pos[s, 1] > RIM, 0, HALF))
            few = extra.at[at] if at >= 4 else extra.at[at, :, :, pl.ds(0, HALF)]
            return (
                pltpu.make_async_copy(image.at[:, pl.ds(base, W), cols], bufs[at], sems.at[at, 0]),
                pltpu.make_async_copy(image.at[:, pl.ds(more, 8), cols], few, sems.at[at, 1]),
            )

        def rim_copy(at, s, source):
            return pltpu.make_async_copy(source.at[s], rim.at[at], sems.at[at, 2])

        def put(at, s):
            return pltpu.make_async_copy(bufs[at], outs[at], sems.at[at, 3])

        def each(job):
            for at in range(8):
                second, k = divmod(at, 4)
                owner = (group + k) % 4
                pl.when(is_owner(owner, second))(
                    lambda at=at, owner=owner, second=second: job(at, slot_of(owner, second))
                )

        def begin(at, s):
            for copy in transfers(at, s):
                copy.start()

            @pl.when(pos[s, 1] > RIM)
            def _():
                rim_copy(at, s, from_right).start()

            @pl.when(pos[s, 1] <= RIM)
            def _():
                rim_copy(at, s, from_left).start()

        def work(at, s):
            for copy in transfers(at, s):
                copy.wait()
            edge = pos[s, 1] - RIM
            out = bufs[at]
            width = out.shape[-1]
            mask = rows_below(pos[s, 0] % 8, (2, 8, width))
            out[:, 0:8, :] = jnp.where(mask, extra[at, :, :, :width], out[:, 0:8, :])
            lane = lax.broadcasted_iota(jnp.int32, (W, HALF), 1)
            low, high = slice(0, HALF), slice(width - HALF, width)

            @pl.when(edge > 0)
            def _():
                rim_copy(at, s, from_right).wait()
                kept = (lane < widths[0, 1]) & (tile < tiles - 1)
                for part in range(2):
                    value = jnp.where(kept, rim[at, part], 1.0 - part)
                    out[part, :, low] = jnp.where(lane < edge, value, out[part, :, low])

            @pl.when(edge <= 0)
            def _():
                rim_copy(at, s, from_left).wait()
                kept = (lane >= HALF - widths[0, 0]) & (tile > 0)
                for part in range(2):
                    value = jnp.where(kept, rim[at, part], 1.0 - part)
                    out[part, :, high] = jnp.where(lane >= HALF + edge, value, out[part, :, high])

            put(at, s).start()

        each(begin)
        each(work)
        each(lambda at, s: put(at, s).wait())

    return pl.pallas_call(
        kernel,
        out_shape=(STRIP,) * 4 + (FIELD,) * 4,
        in_specs=[SMEM_SPEC, SMEM_SPEC, ANY_SPEC, ANY_SPEC, ANY_SPEC],
        out_specs=(ANY_SPEC,) * 8,
        scratch_shapes=[pltpu.VMEM((2, W, HALF), F32)] * 4
        + [pltpu.VMEM((2, W, W), F32)] * 4
        + [
            pltpu.VMEM((8, 2, 8, W), F32),
            pltpu.VMEM((8, 2, W, HALF), F32),
            pltpu.SemaphoreType.DMA((8, 4)),
        ],
        compiler_params=params(),
        cost_estimate=cost(5),
        name="mixed_windows",
    )


class Windows:
    def __init__(self, refs, buf, right, sems):
        self.refs, self.buf, self.sems = refs, buf, sems
        self.at = jnp.where(right, HALF, 0)

    def copies(self, k, n):
        out = self.buf.at[n]
        if len(self.refs) == 4:
            return [pltpu.make_async_copy(self.refs[k], out, self.sems.at[n, 0])]
        pure, mixed = self.refs[k], self.refs[4 + k]
        return [
            pltpu.make_async_copy(pure, out.at[:, :, aligned(self.at)], self.sems.at[n, 0]),
            pltpu.make_async_copy(mixed, out.at[:, :, aligned(HALF - self.at)], self.sems.at[n, 1]),
        ]

    def start(self, first):
        for k in range(4):
            n = (lax.axis_index("cuts") - k) % 4

            @pl.when((n == 0) if first else (n != 0))
            def _(k=k, n=n):
                for copy in self.copies(k, n):
                    copy.start()

    def wait(self, n):
        for copy in self.copies(0, n):
            copy.wait()


class Loads:
    def __init__(self, refs, bufs, sems):
        self.copies = [
            pltpu.make_async_copy(ref, buf, sems.at[at])
            for at, (ref, buf) in enumerate(zip(refs, bufs))
        ]
        for copy in self.copies:
            copy.start()

    def wait(self, *which):
        for at in which:
            self.copies[at].wait()


CONSTANTS = [
    pltpu.VMEM((2, W, W), F32),
    pltpu.VMEM((8, W, W), BF16),
    pltpu.VMEM((2, W, W), F32),
    pltpu.VMEM((W, W), BF16),
    pltpu.VMEM((W, W), BF16),
    pltpu.SemaphoreType.DMA((5,)),
]


def place_probe(probe, row, col, scale, out):
    for part in range(2):
        rolled = pltpu.roll(probe[part], (col - RIM) % W, 1)
        out[part] = pltpu.roll(rolled, row % 8, 0) * scale


def forward_steps(wins, in_buf, kern, tab):
    def step(n, carry):
        wins.wait(n)
        re, im = in_buf[n, 0], in_buf[n, 1]
        wr, wi = wins.buf[n, 0], wins.buf[n, 1]
        re, im = wr * re - wi * im, wr * im + wi * re
        re, im = propagate(re, im, kern, tab, 1.0)
        in_buf[n + 1, 0] = re
        in_buf[n + 1, 1] = im
        return carry

    lax.fori_loop(0, 4, step, 0)


def far_step(in_buf, seen, order, order_t, tab, back):
    half_seen = dot(order[...], seen[...]).astype(BF16)
    target = dot(half_seen, order_t[...])
    spectra = to_spectrum(in_buf[4, 0], in_buf[4, 1], tab)
    chis = []
    for odd in range(2):
        re, im = spectra[odd][:, :HALF], spectra[odd][:, HALF:]
        excess = re * re + im * im - target[:, odd * HALF : (odd + 1) * HALF]
        chis.append(jnp.concatenate([re * excess, im * excess], 1))
    re, im = from_spectrum(chis[0], chis[1], tab)
    back[0] = re
    back[1] = im


def backward_steps(wins, turned_buf, back, kern, tab, store, fresh):
    def step(at, carry):
        n = 3 - at
        re, im = propagate(back[0], back[1], kern, tab, -1.0)
        turned_buf[n, 0] = re
        turned_buf[n, 1] = im
        for k in range(4):
            pl.when((lax.axis_index("cuts") + k) % 4 == n)(lambda k=k: store(k, n).start())
        if fresh:
            wins.wait(n)
        wr, wi = wins.buf[n, 0], wins.buf[n, 1]
        back[0] = wr * re + wi * im
        back[1] = wr * im - wi * re
        return carry

    lax.fori_loop(0, 4, step, 0)


def forward_first():
    def kernel(pos, counts, probe, measured, kern, tab, order, order_t, *rest):
        refs, inputs, back = rest[:8], rest[8:12], rest[12]
        win_buf, in_buf, seen, load_sems, sems, *held = rest[13:]
        group = lax.axis_index("cuts")
        s = slot_of(group, 0)
        *bufs, const_sems = held
        consts = Loads((probe, tab, kern, order, order_t), bufs, const_sems)
        probe, tab, kern, order, order_t = bufs
        wins = Windows(refs, win_buf, pos[s, 1] > RIM, load_sems)
        wins.start(True)
        seeing = pltpu.make_async_copy(measured.at[s], seen, sems.at[4])
        seeing.start()
        consts.wait(0)
        place_probe(probe, pos[s, 0], pos[s, 1], jnp.where(s < counts[0], 1.0, 0.0), in_buf.at[0])
        consts.wait(1, 2)
        wins.start(False)
        forward_steps(wins, in_buf, kern, tab)
        stores = [
            pltpu.make_async_copy(in_buf.at[(group + k) % 4], inputs[k], sems.at[k])
            for k in range(4)
        ]
        for copy in stores:
            copy.start()
        seeing.wait()
        consts.wait(3, 4)
        far_step(in_buf, seen, order, order_t, tab, back)
        for copy in stores:
            copy.wait()

    return pl.pallas_call(
        kernel,
        out_shape=(FIELD,) * 5,
        in_specs=[SMEM_SPEC, SMEM_SPEC] + [ANY_SPEC] * 14,
        out_specs=(ANY_SPEC,) * 4 + (VMEM_SPEC,),
        scratch_shapes=[
            pltpu.VMEM((4, 2, W, W), F32),
            pltpu.VMEM((5, 2, W, W), F32),
            pltpu.VMEM((W, W), BF16),
            pltpu.SemaphoreType.DMA((4, 2)),
            pltpu.SemaphoreType.DMA((5,)),
            *CONSTANTS,
        ],
        compiler_params=params(),
        cost_estimate=cost(9),
        name="forward_first",
    )


def backward_first():
    def kernel(pos, back, kern, tab, *rest):
        refs, turned = rest[:8], rest[8:12]
        win_buf, turned_buf, back_buf, load_sems, sems, *held = rest[12:]
        s = slot_of(lax.axis_index("cuts"), 0)
        *bufs, const_sems = held
        consts = Loads((back, tab, kern), (back_buf, *bufs), const_sems)
        tab, kern = bufs
        wins = Windows(refs, win_buf, pos[s, 1] > RIM, load_sems)
        consts.wait(0, 1, 2)
        wins.start(True)
        wins.start(False)


        def store(k, n):
            return pltpu.make_async_copy(turned_buf.at[n], turned[k], sems.at[k])

        backward_steps(wins, turned_buf, back_buf, kern, tab, store, True)
        for k in range(4):
            store(k, 0).wait()

    return pl.pallas_call(
        kernel,
        out_shape=(FIELD,) * 4,
        in_specs=[SMEM_SPEC] + [ANY_SPEC] * 11,
        out_specs=(ANY_SPEC,) * 4,
        scratch_shapes=[
            pltpu.VMEM((4, 2, W, W), F32),
            pltpu.VMEM((4, 2, W, W), F32),
            pltpu.VMEM((2, W, W), F32),
            pltpu.SemaphoreType.DMA((4, 2)),
            pltpu.SemaphoreType.DMA((4,)),
            pltpu.VMEM((8, W, W), BF16),
            pltpu.VMEM((2, W, W), F32),
            pltpu.SemaphoreType.DMA((3,)),
        ],
        compiler_params=params(),
        cost_estimate=cost(7),
        name="backward_first",
    )


def both_ways(second):
    count = 4 if second else 8

    def kernel(pos, counts, probe, measured, kern, tab, order, order_t, *rest):
        refs, outs = rest[:count], rest[count : count + 4]
        win_buf, in_buf, turned_buf, back_buf, seen, load_sems, sems, *held = rest[count + 4 :]
        group = lax.axis_index("cuts")
        s = slot_of(group, second)

        def store(k, n):
            return pltpu.make_async_copy(turned_buf.at[n], outs[k].at[1], sems.at[4 + k])

        @pl.when(is_owner(group, second))
        def _():
            *bufs, const_sems = held
            consts = Loads((probe, tab, kern, order, order_t), bufs, const_sems)
            probe_buf, tab_buf, kern_buf, order_buf, order_t_buf = bufs
            wins = Windows(refs, win_buf, pos[s, 1] > RIM, load_sems)
            wins.start(True)
            seeing = pltpu.make_async_copy(measured.at[s], seen, sems.at[8])
            seeing.start()
            scale = jnp.where(s < counts[0], 1.0, 0.0)
            consts.wait(0)
            place_probe(probe_buf, pos[s, 0], pos[s, 1], scale, in_buf.at[0])
            consts.wait(1, 2)
            wins.start(False)
            forward_steps(wins, in_buf, kern_buf, tab_buf)
            stores = [
                pltpu.make_async_copy(in_buf.at[(group + k) % 4], outs[k].at[0], sems.at[k])
                for k in range(4)
            ]
            for copy in stores:
                copy.start()
            seeing.wait()
            consts.wait(3, 4)
            far_step(in_buf, seen, order_buf, order_t_buf, tab_buf, back_buf)
            backward_steps(wins, turned_buf, back_buf, kern_buf, tab_buf, store, False)
            for copy in stores:
                copy.wait()
            for k in range(4):
                store(k, 0).wait()

    pair = jax.ShapeDtypeStruct((2, 2, W, W), F32)
    return pl.pallas_call(
        kernel,
        out_shape=(pair,) * 4,
        in_specs=[SMEM_SPEC, SMEM_SPEC] + [ANY_SPEC] * (6 + count),
        out_specs=(ANY_SPEC,) * 4,
        scratch_shapes=[
            pltpu.VMEM((4, 2, W, W), F32),
            pltpu.VMEM((5, 2, W, W), F32),
            pltpu.VMEM((4, 2, W, W), F32),
            pltpu.VMEM((2, W, W), F32),
            pltpu.VMEM((W, W), BF16),
            pltpu.SemaphoreType.DMA((4, 2)),
            pltpu.SemaphoreType.DMA((9,)),
            *CONSTANTS,
        ],
        compiler_params=params(),
        cost_estimate=cost(14),
        name="both_second" if second else "both_first",
    )


def each_owner(second, job):
    for j in range(4):
        owner = (lax.axis_index("cuts") - j) % 4
        pl.when(is_owner(owner, second))(lambda j=j, owner=owner: job(j, slot_of(owner, second)))


def adjoint_of(t_buf, w_buf, pos, s, out):
    re, im = t_buf[0], t_buf[1]
    wr, wi = w_buf[0], w_buf[1]
    for part, value in enumerate((wr * re + wi * im, wr * im - wi * re)):
        rolled = pltpu.roll(value, (W + RIM - pos[s, 1]) % W, 1)
        out[part] = pltpu.roll(rolled, (W - pos[s, 0] % 8) % W, 0)


def conj_terms(i_buf, t_buf, half):
    ir, ii = i_buf[0, :, half], i_buf[1, :, half]
    re, im = t_buf[0, :, half], t_buf[1, :, half]
    return ir * re + ii * im, ir * im - ii * re


LOW, HIGH = slice(0, HALF), slice(HALF, W)


def lanes():
    return lax.broadcasted_iota(jnp.int32, (W, HALF), 1)


def rim_terms(i_buf, t_buf, edge, widths, to_left, to_right):
    tile, tiles = lax.axis_index("tile"), lax.axis_size("tile")
    lane = lanes()
    sent_left = (lane >= HALF + edge) & (lane >= HALF - widths[0, 0]) & (tile > 0)
    sent_right = (lane < edge) & (lane < widths[0, 1]) & (tile < tiles - 1)

    @pl.when(edge > 0)
    def _():
        for part, value in enumerate(conj_terms(i_buf, t_buf, LOW)):
            to_right[part] = jnp.where(sent_right, value, 0.0)
            to_left[part] = jnp.zeros_like(value)

    @pl.when(edge <= 0)
    def _():
        for part, value in enumerate(conj_terms(i_buf, t_buf, HIGH)):
            to_left[part] = jnp.where(sent_left, value, 0.0)
            to_right[part] = jnp.zeros_like(value)


def own_terms(i_buf, t_buf, edge):
    lane = lanes()
    low = [jnp.where(lane < edge, 0.0, value) for value in conj_terms(i_buf, t_buf, LOW)]
    high = [jnp.where(lane >= HALF + edge, 0.0, value) for value in conj_terms(i_buf, t_buf, HIGH)]
    return low, high


def terms_first(cap):
    def kernel(pos, counts, widths, probe, *rest):
        inputs, turned, pure, mixed = rest[:4], rest[4:8], rest[8:12], rest[12:16]
        adjoint, own, to_left, to_right = rest[16:20]
        buf, w_buf, a_buf, sems = rest[20:]

        def loads(j, s):
            k = (4 - j) % 4
            at = jnp.where(pos[s, 1] > RIM, HALF, 0)
            out = w_buf.at[j]
            return (
                pltpu.make_async_copy(inputs[j], buf.at[j, 0], sems.at[j, 0]),
                pltpu.make_async_copy(turned[j], buf.at[j, 1], sems.at[j, 1]),
                pltpu.make_async_copy(pure[k], out.at[:, :, aligned(at)], sems.at[j, 2]),
                pltpu.make_async_copy(mixed[k], out.at[:, :, aligned(HALF - at)], sems.at[j, 3]),
            )

        def store(j, s):
            return pltpu.make_async_copy(a_buf.at[j], adjoint.at[s], sems.at[j, 4])

        def begin(j, s):
            for copy in loads(j, s):
                copy.start()

        def work(j, s):
            for copy in loads(j, s):
                copy.wait()
            edge = pos[s, 1] - RIM

            @pl.when(lax.axis_index("cuts") == 0)
            def _():
                scale = jnp.where(s < counts[0], 1.0, 0.0)
                place_probe(probe, pos[s, 0], pos[s, 1], scale, buf.at[j, 0])

            ins, outs = buf.at[j, 0], buf.at[j, 1]
            rim_terms(ins, outs, edge, widths, to_left.at[s], to_right.at[s])
            for half, values in zip((LOW, HIGH), own_terms(ins, outs, edge)):
                for part, value in enumerate(values):
                    own[s, part, :, half] = value
            adjoint_of(outs, w_buf.at[j], pos, s, a_buf.at[j])
            store(j, s).start()

        each_owner(0, begin)
        each_owner(0, work)
        each_owner(0, lambda j, s: store(j, s).wait())

    strips = jax.ShapeDtypeStruct((4, 2, W, HALF), F32)
    return pl.pallas_call(
        kernel,
        out_shape=(
            jax.ShapeDtypeStruct((cap, 2, W, W), F32),
            jax.ShapeDtypeStruct((4, 2, W, W), F32),
            strips,
            strips,
        ),
        in_specs=[SMEM_SPEC] * 3 + [VMEM_SPEC] + [ANY_SPEC] * 16,
        out_specs=(ANY_SPEC, VMEM_SPEC, VMEM_SPEC, VMEM_SPEC),
        scratch_shapes=[
            pltpu.VMEM((4, 2, 2, W, W), F32),
            pltpu.VMEM((4, 2, W, W), F32),
            pltpu.VMEM((4, 2, W, W), F32),
            pltpu.SemaphoreType.DMA((4, 5)),
        ],
        compiler_params=params(),
        cost_estimate=cost(7),
        name="terms_first",
    )


def rims_second(count):
    def kernel(pos, counts, widths, probe, *rest):
        pairs, (to_left, to_right), (buf, sems) = rest[:4], rest[4:6], rest[6:]

        def load(j):
            return pltpu.make_async_copy(pairs[j], buf.at[j], sems.at[j])

        def work(j, s):
            load(j).wait()

            @pl.when(lax.axis_index("cuts") == 0)
            def _():
                scale = jnp.where(s < counts[0], 1.0, 0.0)
                place_probe(probe, pos[s, 0], pos[s, 1], scale, buf.at[j, 0])

            edge = pos[s, 1] - RIM
            at = s - 4
            rim_terms(buf.at[j, 0], buf.at[j, 1], edge, widths, to_left.at[at], to_right.at[at])

        each_owner(1, lambda j, s: load(j).start())
        each_owner(1, work)

    strips = jax.ShapeDtypeStruct((count, 2, W, HALF), F32)
    return pl.pallas_call(
        kernel,
        out_shape=(strips, strips),
        in_specs=[SMEM_SPEC] * 3 + [VMEM_SPEC] + [ANY_SPEC] * 4,
        out_specs=(VMEM_SPEC, VMEM_SPEC),
        scratch_shapes=[pltpu.VMEM((4, 2, 2, W, W), F32), pltpu.SemaphoreType.DMA((4,))],
        compiler_params=params(),
        cost_estimate=cost(3),
        name="rims_second",
    )


class AddInto:
    def __init__(self, grad, row, cols, buf, more_buf, sems):
        base, more, self.delta = row_base(row)
        self.buf, self.more_buf = buf, more_buf
        self.pairs = (
            (grad.at[:, pl.ds(base, W), cols], buf),
            (grad.at[:, pl.ds(more, 8), cols], more_buf),
        )
        self.sems = sems

    def copies(self, inward):
        return [
            pltpu.make_async_copy(
                pair[0 if inward else 1], pair[1 if inward else 0], self.sems.at[at]
            )
            for at, pair in enumerate(self.pairs)
        ]

    def start(self, inward):
        for copy in self.copies(inward):
            copy.start()

    def wait(self, inward):
        for copy in self.copies(inward):
            copy.wait()

    def add(self, part, half, value):
        below = rows_below(self.delta, value.shape)
        self.buf[part, :, half] += jnp.where(below, 0.0, value)
        few = rows_below(self.delta, value[:8].shape)
        self.more_buf[part, :, half] += jnp.where(few, value[:8], 0.0)


def add_rows(out, row, value, cols):
    base, more, delta = row_base(row)
    width = value[0].shape[-1]
    below = rows_below(delta, (W, width))
    few = rows_below(delta, (8, width))
    for part in range(2):
        out[part, pl.ds(base, W), cols] += jnp.where(below, 0.0, value[part])
        out[part, pl.ds(more, 8), cols] += jnp.where(few, value[part][:8], 0.0)


def finish(cap, rows):
    def kernel(pos, pos_left, pos_right, counts, probe, own, left, right, adjoint_in, *rest):
        pairs, full, (adjoint, grad) = rest[:4], rest[4:8], rest[8:10]
        buf, w_buf, a_buf, sems = rest[10:]

        def loads(j):
            return (
                pltpu.make_async_copy(pairs[j], buf.at[j], sems.at[j, 0]),
                pltpu.make_async_copy(full[(4 - j) % 4], w_buf.at[j], sems.at[j, 1]),
            )

        def store(j, s):
            return pltpu.make_async_copy(a_buf.at[j], adjoint.at[s], sems.at[j, 2])

        def begin(j, s):
            for copy in loads(j):
                copy.start()

        def work(j, s):
            for copy in loads(j):
                copy.wait()

            @pl.when(lax.axis_index("cuts") == 0)
            def _():
                scale = jnp.where(s < counts[0], 1.0, 0.0)
                place_probe(probe, pos[s, 0], pos[s, 1], scale, buf.at[j, 0])

            adjoint_of(buf.at[j, 1], w_buf.at[j], pos, s, a_buf.at[j])
            store(j, s).start()
            terms = own_terms(buf.at[j, 0], buf.at[j, 1], pos[s, 1] - RIM)
            for half, values in zip((LOW, HIGH), terms):
                add_rows(grad, pos[s, 0], values, half)

        each_owner(1, begin)
        grad[...] = jnp.zeros_like(grad)
        for s in range(4):
            add_rows(grad, pos[s, 0], own[s], slice(0, W))
            add_rows(grad, pos_left[s, 0], left[s], LOW)
            add_rows(grad, pos_right[s, 0], right[s], HIGH)
        each_owner(1, work)
        each_owner(1, lambda j, s: store(j, s).wait())

    return pl.pallas_call(
        kernel,
        out_shape=(
            jax.ShapeDtypeStruct((cap, 2, W, W), F32),
            jax.ShapeDtypeStruct((2, rows, W), F32),
        ),
        in_specs=[SMEM_SPEC] * 4 + [VMEM_SPEC] * 4 + [ANY_SPEC] * 9,
        out_specs=(ANY_SPEC, VMEM_SPEC),
        scratch_shapes=[
            pltpu.VMEM((4, 2, 2, W, W), F32),
            pltpu.VMEM((4, 2, W, W), F32),
            pltpu.VMEM((4, 2, W, W), F32),
            pltpu.SemaphoreType.DMA((4, 3)),
        ],
        input_output_aliases={8: 0},
        compiler_params=params(),
        cost_estimate=cost(9),
        name="finish",
    )


def add_rims(count, rows):
    def kernel(pos_left, pos_right, grad_in, left, right, grad, buf, more_buf, sems):
        sides = ((pos_left, left), (pos_right, right))

        def adder(s, side):
            row, cols = sides[side][0][4 + s, 0], pl.ds(side * HALF, HALF)
            return AddInto(
                grad, row, cols, buf.at[s, side], more_buf.at[s, side], sems.at[s, side]
            )

        def add_slots(slots):
            adders = [(s, side, adder(s, side)) for s in slots for side in range(2)]
            for _, _, add in adders:
                add.start(True)
            for s, side, add in adders:
                add.wait(True)
                for part in range(2):
                    add.add(part, LOW, sides[side][1][s, part])
                add.start(False)
            for _, _, add in adders:
                add.wait(False)

        apart = jnp.bool_(True)
        for pos, _ in sides:
            for one in range(count):
                for two in range(one):
                    apart &= jnp.abs(pos[4 + one, 0] - pos[4 + two, 0]) >= W + 32

        @pl.when(apart)
        def _():
            add_slots(range(count))

        @pl.when(jnp.logical_not(apart))
        def _():
            for s in range(count):
                add_slots([s])

    return pl.pallas_call(
        kernel,
        out_shape=jax.ShapeDtypeStruct((2, rows, W), F32),
        in_specs=[SMEM_SPEC] * 2 + [ANY_SPEC] + [VMEM_SPEC] * 2,
        out_specs=ANY_SPEC,
        scratch_shapes=[
            pltpu.VMEM((count, 2, 2, W, HALF), F32),
            pltpu.VMEM((count, 2, 2, 8, HALF), F32),
            pltpu.SemaphoreType.DMA((count, 2, 2)),
        ],
        input_output_aliases={2: 0},
        compiler_params=params(),
        cost_estimate=cost(4),
        name="add_rims",
    )


def after(value, *others):
    return lax.optimization_barrier((value, *others))[0]


def on_device(probe_wave, transmission, kernel_phase, measured, counts, positions, widths):
    groups, tiles = lax.axis_size("cuts"), lax.axis_size("tile")
    cap = positions.shape[1]
    rows = transmission.shape[2]
    image, pos = transmission[0], positions[0]
    up = [(i, i + 1) for i in range(tiles - 1)]
    down = [(i + 1, i) for i in range(tiles - 1)]

    def to_up(value):
        return lax.ppermute(value, "tile", up)

    def to_down(value):
        return lax.ppermute(value, "tile", down)

    def shift(value, by, keep):
        pairs = [
            (g * tiles + t, (g + by) % groups * tiles + t)
            for g in range(groups)
            for t in range(tiles)
            if keep(g, (g + by) % groups, t % 2)
        ]
        return lax.ppermute(value, ("cuts", "tile"), pairs)

    def shifted(values, keep):
        moved = {k: shift(values[k], k, keep) for k in (1, 3, 2)}
        return [values[0], moved[1], moved[2], moved[3]]

    every = lambda src, dst, parity: True
    to_owner = lambda src, dst, parity: dst % 2 == parity
    inner = lambda src, dst, parity: dst != 0
    owned = lambda src, dst, parity: src % 2 == parity

    order = jnp.asarray(ORDER)
    exact = lax.Precision.HIGHEST
    phase = jnp.dot(jnp.dot(order, kernel_phase, precision=exact), order.T, precision=exact)
    kern = jnp.stack([jnp.cos(phase), jnp.sin(phase)])
    tab = jnp.asarray(TABLES)
    hot, hot_t = order.astype(BF16), order.T.astype(BF16)

    pos_left, pos_right = to_up(pos), to_down(pos)
    pure1 = pure_halves()(pos, image)
    got_pure1 = shifted(pure1, every)
    edge_left, edge_right = cut_rims(cap)(pos_left, pos_right, image)
    rim_right, rim_left = to_down(edge_left), to_up(edge_right)
    rim_left = after(rim_left, kern, *got_pure1[1:])

    made = mixed_windows()(pos, widths, image, rim_left, rim_right)
    mixed1, full2 = made[:4], made[4:]
    got_mixed1 = shifted(mixed1, every)
    got_full2 = shifted([after(value, *got_mixed1[1:]) for value in full2], to_owner)

    wide = (probe_wave, measured[0], kern, tab, hot, hot_t)
    *in1, back1 = forward_first()(pos, counts, *wide, *got_pure1, *got_mixed1)
    got_in1 = shifted(in1, inner)
    back1 = after(back1, *got_full2[1:])
    turned1 = backward_first()(pos, back1, kern, tab, *got_pure1, *got_mixed1)
    got_turned1 = shifted(turned1, every)
    got_full2[0] = after(got_full2[0], turned1[1], got_in1[1])
    pairs2 = both_ways(1)(pos, counts, *wide, *got_full2)
    got_pairs2 = shifted(pairs2, owned)

    adjoint, own1, left1, right1 = terms_first(cap)(
        pos, counts, widths, probe_wave, *got_in1, *got_turned1, *pure1, *mixed1
    )
    right1, left1 = to_down(left1), to_up(right1)
    left2, right2 = rims_second(cap - 4)(pos, counts, widths, probe_wave, *got_pairs2)
    own1 = after(own1, left2)
    right2, left2 = to_down(left2), to_up(right2)
    adjoint, grad = finish(cap, rows)(
        pos, pos_left, pos_right, counts, probe_wave, own1, left1, right1, adjoint,
        *got_pairs2, *full2
    )
    grad = add_rims(cap - 4, rows)(pos_left, pos_right, grad, left2, right2)
    return adjoint[None, None], grad[None]


def solution(mesh):
    return jax.shard_map(
        on_device,
        mesh=mesh,
        in_specs=(
            P(),
            P("cuts", None, None, "tile"),
            P(),
            P("tile", None, None, None),
            P("tile"),
            P("tile", None, None),
            P("tile", None),
        ),
        out_specs=(P("cuts", "tile", None, None, None, None), P("cuts", None, None, "tile")),
        check_vma=False,
    )
```
